256 devices in a mesh: grp: 8 (over x, core), seq: 32 (over z, y).
Axes of the slice: x: 4, y: 4, z: 8, core: 2. Of those that a mesh axis runs over, the one named last changes fastest.
Arguments:
- queries: bfloat16 [8, 3, 32, 128, 512], P('grp', None, 'seq'), may hold values from -120 to 120
- key_input: bfloat16 [8, 3, 32, 128, 512], P('grp', None, 'seq'), may hold values from -8 to 8
- value_input: bfloat16 [8, 3, 32, 128, 512], P('grp', None, 'seq'), may hold values from -6 to 6
- grad_output: bfloat16 [8, 3, 32, 128, 512], P('grp', None, 'seq'), may hold values from -6 to 6
- block_lists: int32 [768, 16], replicated, may hold values from -1 to 767, as said below
- block_flags: int32 [768, 16], replicated, may hold values from 0 to 1, as said below
Outputs:
- attended: bfloat16 [8, 3, 32, 128, 512], P('grp', None, 'seq')
- grad_queries: bfloat16 [8, 3, 32, 128, 512], P('grp', None, 'seq')
- grad_keys: bfloat16 [8, 3, 32, 128, 512], P('grp', None, 'seq')
- grad_values: bfloat16 [8, 3, 32, 128, 512], P('grp', None, 'seq')
The draws below stay inside these ranges and needn't reach their ends.
Inputs may be any that keep to these rules, and one draw needn't show every extreme that they name: `block_lists`: entry 0 of row t is t itself; the other used entries of a row are distinct tiles u < t, each either in the same block of 96 tiles as t, or in an earlier block with u % 32 == t % 32; used entries come first and -1 fills the rest. The 3 rows t = (a * 3 + b) * 32 + c that share a and c name together at most one tile of the form (a2 * 3 + b2) * 32 + c2 for each pair (a2, c2) other than (a, c). block_flags[t, 0] is 1 for every t; a flag whose list entry is -1 has no effect.
All inputs are finite; a program needn't handle non-finite values.
Results may differ from the reference program's by a relative error of at most 0.029.
Values may be sent and summed in bfloat16 or wider, within the bound.
No kernel may reach another device: no remote copies, remote signals or barrier semaphores. Data moves between devices by JAX's collectives and lax.ppermute only.
A program may use at most 256 MiB of HBM per device.

```python
import jax
import jax.numpy as jnp
from jax import lax

HEADS = 8
HEAD_DIM = 64
TILE = 128
TILE_DEV = 3
GROUPS = 8
COLUMNS = 32
LIST = 16
WIDTH = 512
TILES = 768


def key_field(key):
    base_draw = 1.6 * jax.random.normal(jax.random.fold_in(key, 31), (GROUPS, TILE_DEV, COLUMNS, TILE, WIDTH), jnp.float32)
    base_draw = jnp.clip(base_draw, -8.0, 8.0)
    return base_draw


def draw_key_input(key, part):
    return key_field(key).astype(jnp.bfloat16)


def draw_queries(key, part):
    fresh_draw = 1.6 * jax.random.normal(jax.random.fold_in(key, 32), (GROUPS, TILE_DEV, COLUMNS, TILE, WIDTH), jnp.float32)
    fresh_draw = jnp.clip(fresh_draw, -8.0, 8.0)
    return fresh_draw.astype(jnp.bfloat16)


def draw_block_lists(key, part):
    group_tiles = TILE_DEV * COLUMNS
    shape = (GROUPS, TILE_DEV, COLUMNS)
    streams = jax.random.split(jax.random.fold_in(key, 41), 6)
    peer_rank = jax.random.randint(streams[0], (GROUPS, 1, COLUMNS, COLUMNS), 0, TILE_DEV)
    far_rank = jax.random.randint(streams[1], (GROUPS, 1, COLUMNS, GROUPS), 0, TILE_DEV)
    full_column = jax.random.randint(streams[2], (GROUPS, 1, 1, 1), min(LIST - 1, COLUMNS - 1), COLUMNS)
    peer_coin = jax.random.randint(streams[3], (GROUPS, TILE_DEV, COLUMNS, COLUMNS), 0, 2)
    far_coin = jax.random.randint(streams[4], (GROUPS, TILE_DEV, COLUMNS, GROUPS), 0, 4)
    own_coin = jax.random.randint(streams[5], (GROUPS, TILE_DEV, COLUMNS, TILE_DEV), 0, 2)
    group_at = jnp.arange(GROUPS, dtype=jnp.int32).reshape(GROUPS, 1, 1, 1)
    rank_at = jnp.arange(TILE_DEV, dtype=jnp.int32).reshape(1, TILE_DEV, 1, 1)
    column_at = jnp.arange(COLUMNS, dtype=jnp.int32).reshape(1, 1, COLUMNS, 1)
    local_at = rank_at * COLUMNS + column_at
    tile_at = group_at * group_tiles + local_at
    full_device = column_at == full_column
    full_tile = full_device & (rank_at == TILE_DEV - 1)
    other_rank = jnp.arange(TILE_DEV, dtype=jnp.int32).reshape(1, 1, 1, TILE_DEV)
    own_ids = group_at * group_tiles + other_rank * COLUMNS + column_at
    own_take = (other_rank < rank_at) & (own_coin == 1)
    other_group = jnp.arange(GROUPS, dtype=jnp.int32).reshape(1, 1, 1, GROUPS)
    far_ids = other_group * group_tiles + far_rank * COLUMNS + column_at
    far_take = (other_group < group_at) & ((far_coin > 0) | full_tile)
    peer_at = jnp.arange(COLUMNS, dtype=jnp.int32).reshape(1, 1, 1, COLUMNS)
    chosen = jnp.where(full_device & (peer_at > column_at), 0, peer_rank)
    peer_local = chosen * COLUMNS + peer_at
    peer_ids = group_at * group_tiles + peer_local
    peer_take = (peer_at != column_at) & (peer_local < local_at) & ((peer_coin == 1) | full_tile)
    entry_ids = jnp.concatenate([jnp.broadcast_to(tile_at, shape + (1,)), jnp.broadcast_to(own_ids, shape + (TILE_DEV,)), jnp.broadcast_to(far_ids, shape + (GROUPS,)), jnp.broadcast_to(peer_ids, shape + (COLUMNS,))], axis=3)
    taken = jnp.concatenate([jnp.ones(shape + (1,), bool), jnp.broadcast_to(own_take, shape + (TILE_DEV,)), jnp.broadcast_to(far_take, shape + (GROUPS,)), jnp.broadcast_to(peer_take, shape + (COLUMNS,))], axis=3)
    candidates = 1 + TILE_DEV + GROUPS + COLUMNS
    position = jnp.arange(candidates, dtype=jnp.int32)
    order = jnp.argsort(jnp.where(taken, position, candidates + position), axis=3)[..., :LIST]
    picked_ids = jnp.take_along_axis(entry_ids, order, axis=3)
    picked_taken = jnp.take_along_axis(taken, order, axis=3)
    return jnp.where(picked_taken, picked_ids, -1).reshape(TILES, LIST).astype(jnp.int32)


def draw_block_flags(key, part):
    coins = jax.random.randint(jax.random.fold_in(key, 51), (TILES, LIST), 0, 2)
    leading_entry = (jnp.arange(LIST) == 0)[None, :]
    return jnp.where(leading_entry, 1, coins).astype(jnp.int32)


def steps_of(key, dims, cuts, low, high):
    def one(axis_at, blocks):
        draws = jax.random.uniform(jax.random.fold_in(jax.random.fold_in(key, 6), axis_at), (blocks,), jnp.float32, low / len(cuts), high / len(cuts))
        return jnp.repeat(jnp.exp(draws), dims[axis_at] // blocks).reshape((-1,) + (1,) * (len(dims) - axis_at - 1))

    factor_of = one(*cuts[0])
    for cut in cuts[1:]:
        factor_of = factor_of * one(*cut)
    return factor_of


def noise(key, shape, scale, limit, pieces=(), kind=jnp.bfloat16):
    result = scale * jax.random.normal(key, shape, jnp.float32)
    if pieces:
        result = result * steps_of(key, shape, pieces, -0.22, 0.18)
    return jnp.clip(result, -limit, limit).astype(kind)


def setup_inputs(seed: int = 0) -> dict:
    arg_keys = jax.random.split(jax.random.key(seed), 7)
    return {
        "queries": draw_queries(jax.random.fold_in(arg_keys[6], 71), 0),
        "key_input": draw_key_input(jax.random.fold_in(arg_keys[6], 71), 0),
        "value_input": noise(arg_keys[2], (GROUPS, TILE_DEV, COLUMNS, TILE, WIDTH), 1.0, 6.0, ((0, 8), (2, 32))),
        "grad_output": noise(arg_keys[3], (GROUPS, TILE_DEV, COLUMNS, TILE, WIDTH), 1.0, 6.0, ((0, 8), (2, 32))),
        "block_lists": draw_block_lists(jax.random.fold_in(arg_keys[6], 71), 0),
        "block_flags": draw_block_flags(jax.random.fold_in(arg_keys[6], 71), 0),
    }


floor_score = -1.0e30


def tile_pass(query_tile, grad_tile, key_group, value_group, present, flag_row):
    tile_rows = query_tile.shape[0]
    entries = key_group.shape[0]
    score_scale = HEAD_DIM ** -0.5
    query_f = query_tile.astype(jnp.float32).reshape(tile_rows, HEADS, HEAD_DIM)
    grad_f = grad_tile.astype(jnp.float32).reshape(tile_rows, HEADS, HEAD_DIM)
    key_f = key_group.astype(jnp.float32).reshape(entries, tile_rows, HEADS, HEAD_DIM)
    value_f = value_group.astype(jnp.float32).reshape(entries, tile_rows, HEADS, HEAD_DIM)
    positions = jnp.arange(tile_rows)
    lower_mask = positions[None, :] <= positions[:, None]
    allowed = present[None, :, None] & ((flag_row == 0)[None, :, None] | lower_mask[:, None, :])
    scores = jnp.einsum("ihd,echd->hiec", query_f, key_f) * score_scale
    masked = jnp.where(allowed[None], scores, floor_score)
    row_top = jnp.max(masked, axis=(2, 3), keepdims=True)
    exponent = jnp.exp(masked - row_top)
    probs_exact = exponent / jnp.sum(exponent, axis=(2, 3), keepdims=True)
    probs_f = lax.optimization_barrier(probs_exact.astype(jnp.bfloat16)).astype(jnp.float32)
    attended_tile = jnp.einsum("hiec,echd->ihd", probs_f, value_f).astype(jnp.bfloat16)
    row_delta = jnp.sum(grad_f * attended_tile.astype(jnp.float32), axis=2)
    dprobs = jnp.einsum("ihd,echd->hiec", grad_f, value_f)
    dscores = probs_exact * (dprobs - jnp.transpose(row_delta)[:, :, None, None])
    dscores = lax.optimization_barrier(dscores.astype(jnp.bfloat16)).astype(jnp.float32)
    grad_query = (jnp.einsum("hiec,echd->ihd", dscores, key_f) * score_scale).astype(jnp.bfloat16)
    grad_key = jnp.einsum("hiec,ihd->echd", dscores, query_f) * score_scale
    grad_value = jnp.einsum("hiec,ihd->echd", probs_f, grad_f)
    return (attended_tile.reshape(tile_rows, WIDTH), grad_query.reshape(tile_rows, WIDTH),
            grad_key.reshape(entries, tile_rows, WIDTH), grad_value.reshape(entries, tile_rows, WIDTH))


def reference(queries, key_input, value_input, grad_output, block_lists, block_flags):
    query_all = queries.reshape(TILES, TILE, WIDTH)
    key_all = key_input.reshape(TILES, TILE, WIDTH)
    value_all = value_input.reshape(TILES, TILE, WIDTH)
    grad_all = grad_output.reshape(TILES, TILE, WIDTH)
    ranks = jnp.arange(TILE_DEV, dtype=jnp.int32)

    def device_step(totals, device_index):
        key_total, value_total = totals
        group_at = device_index // COLUMNS
        column_at = device_index % COLUMNS
        my_tiles = (group_at * TILE_DEV + ranks) * COLUMNS + column_at
        attended_rows = []
        grad_rows = []
        key_terms = []
        value_terms = []
        entry_rows = []
        for rank in range(TILE_DEV):
            tile_at = my_tiles[rank]
            list_row = block_lists[tile_at]
            present = list_row >= 0
            safe_ids = jnp.maximum(list_row, 0).astype(jnp.int32)
            outcome = tile_pass(query_all[tile_at], grad_all[tile_at],
                                jnp.take(key_all, safe_ids, axis=0), jnp.take(value_all, safe_ids, axis=0),
                                present, block_flags[tile_at])
            attended_rows.append(outcome[0])
            grad_rows.append(outcome[1])
            key_terms.append(outcome[2])
            value_terms.append(outcome[3])
            entry_rows.append(list_row)
        entry_ids = jnp.concatenate(entry_rows)
        same_tile = ((entry_ids[:, None] == entry_ids[None, :]) & (entry_ids[None, :] >= 0)).astype(jnp.float32)
        keep_first = ((jnp.sum(jnp.tril(same_tile, -1), axis=1) == 0) & (entry_ids >= 0)).astype(jnp.float32)

        def partial_sum(terms):
            summed = jnp.einsum("ab,btw->atw", same_tile, jnp.concatenate(terms), precision=lax.Precision.HIGHEST)
            rounded = lax.optimization_barrier(summed.astype(jnp.bfloat16)).astype(jnp.float32)
            return rounded * keep_first[:, None, None]

        target = jnp.maximum(entry_ids, 0).astype(jnp.int32)
        key_total = key_total.at[target].add(partial_sum(key_terms))
        value_total = value_total.at[target].add(partial_sum(value_terms))
        return (key_total, value_total), (jnp.stack(attended_rows), jnp.stack(grad_rows))

    zeros = jnp.zeros((TILES, TILE, WIDTH), jnp.float32)
    totals, stacked = lax.scan(device_step, (zeros, zeros), jnp.arange(GROUPS * COLUMNS, dtype=jnp.int32))

    def arrange(values_out):
        return jnp.transpose(values_out.reshape(GROUPS, COLUMNS, TILE_DEV, TILE, WIDTH), (0, 2, 1, 3, 4))

    grad_keys = totals[0].astype(jnp.bfloat16).reshape(GROUPS, TILE_DEV, COLUMNS, TILE, WIDTH)
    grad_values = totals[1].astype(jnp.bfloat16).reshape(GROUPS, TILE_DEV, COLUMNS, TILE, WIDTH)
    return (arrange(stacked[0]), arrange(stacked[1]), grad_keys, grad_values)
```

```python
import functools

import jax
import jax.numpy as jnp
from jax import lax
from jax.experimental import pallas as pl
from jax.experimental.pallas import tpu as pltpu
from jax.sharding import PartitionSpec as P

HEADS = 8
HEAD_DIM = 64
Y_SIZE = 4
LOG2E = 1.4426950408889634
HIDDEN = -1e30


def pack_kernel(q_ref, k_ref, v_ref, g_ref, kv_ref, qg_ref):
    for head in range(HEADS):
        at = head * HEAD_DIM
        cols = slice(at, at + HEAD_DIM)
        kv_ref[head] = jnp.concatenate([k_ref[:, :, cols], v_ref[:, :, cols]], axis=-1)
        qg_ref[head] = jnp.concatenate([q_ref[:, :, cols], g_ref[:, :, cols]], axis=-1)


def unpack_kernel(in_ref, first_ref, second_ref):
    for pair in range(HEADS // 2):
        even = in_ref[2 * pair]
        odd = in_ref[2 * pair + 1]
        cols = slice(pair * 128, pair * 128 + 128)
        first_ref[:, :, cols] = jnp.concatenate([even[..., :HEAD_DIM], odd[..., :HEAD_DIM]], axis=-1)
        second_ref[:, :, cols] = jnp.concatenate([even[..., HEAD_DIM:], odd[..., HEAD_DIM:]], axis=-1)


def far_kernel(rank_ref, kv_ref, out_ref, *, groups, zs):
    def step(at, carry):
        z = at % zs
        rank = jnp.maximum(rank_ref[at], 0)
        out_ref[at] = kv_ref[z, rank]
        return carry

    lax.fori_loop(0, groups * zs, step, 0)


def attend_kernel(
    code_ref, count_ref, near_ref, far_ref, qg_ref,
    odq_ref, dnear_ref, dfar_ref,
    table, totals, scores, dprobs, masks, weights, sems,
    *, tiles, entries, near, far,
):
    copies = [
        pltpu.make_async_copy(near_ref, table.at[pl.ds(0, near)], sems.at[0]),
        pltpu.make_async_copy(far_ref, table.at[pl.ds(near, far)], sems.at[1]),
    ]
    for copy in copies:
        copy.start()
    rows = 128
    key_at = lax.broadcasted_iota(jnp.int32, (rows, rows), 0)
    query_at = lax.broadcasted_iota(jnp.int32, (rows, rows), 1)
    masks[0] = jnp.zeros((rows, rows), jnp.float32)
    masks[1] = jnp.where(key_at <= query_at, 0.0, HIDDEN).astype(jnp.float32)
    masks[2] = jnp.full((rows, rows), HIDDEN, jnp.float32)
    table[near + far] = jnp.zeros((rows, rows), table.dtype)

    def clear(at, carry):
        totals[at] = jnp.zeros((rows, rows), jnp.float32)
        return carry

    lax.fori_loop(0, near + far + 1, clear, 0)
    for copy in copies:
        copy.wait()
    left = lax.broadcasted_iota(jnp.int32, (rows, rows), 1) < HEAD_DIM
    scale = HEAD_DIM ** -0.5

    def tile_step(tile, carry):
        qg = qg_ref[tile]
        weights[pl.ds(0, rows), :] = jnp.where(left, qg, jnp.zeros_like(qg))
        weights[pl.ds(rows, rows), :] = jnp.where(left, jnp.zeros_like(qg), qg)
        pairs = (count_ref[tile] + 1) // 2

        def score_step(pair, top):
            for half in range(2):
                entry = pair * 2 + half
                code = code_ref[tile * entries + entry]
                kv = table[code // 4]
                both = lax.dot_general(
                    kv, weights[...], (((1,), (1,)), ((), ())), preferred_element_type=jnp.float32
                )
                masked = both[:, :rows] + masks[code % 4]
                scores[entry] = masked
                dprobs[entry] = both[:, rows:]
                top = jnp.maximum(top, jnp.max(masked.reshape(rows // 8, 8, rows), axis=0))
            return top

        top = lax.fori_loop(0, pairs, score_step, jnp.full((8, rows), HIDDEN, jnp.float32))
        row_top = jnp.max(top, axis=0, keepdims=True)

        def exp_step(pair, carry):
            total, mixed = carry
            for half in range(2):
                entry = pair * 2 + half
                prob = jnp.exp2((scores[entry] - row_top) * (scale * LOG2E))
                scores[entry] = prob
                total = total + jnp.sum(prob.reshape(rows // 8, 8, rows), axis=0)
                mixed = mixed + jnp.sum((prob * dprobs[entry]).reshape(rows // 8, 8, rows), axis=0)
            return total, mixed

        zero = jnp.zeros((8, rows), jnp.float32)
        total, mixed = lax.fori_loop(0, pairs, exp_step, (zero, zero))
        inverse = 1.0 / jnp.sum(total, axis=0, keepdims=True)
        delta = jnp.sum(mixed, axis=0, keepdims=True) * inverse

        def grad_step(pair, carry):
            attended, grad_query = carry
            for half in range(2):
                entry = pair * 2 + half
                slot = code_ref[tile * entries + entry] // 4
                prob = scores[entry] * inverse
                dscore = prob * (dprobs[entry] - delta)
                both = jnp.concatenate([dscore, prob], axis=1).astype(jnp.bfloat16)
                totals[slot] = totals[slot] + jnp.dot(
                    both, weights[...], preferred_element_type=jnp.float32
                )
                mixed = lax.dot_general(
                    table[slot], both, (((0,), (0,)), ((), ())), preferred_element_type=jnp.float32
                )
                grad_query = grad_query + mixed[:HEAD_DIM, :rows]
                attended = attended + mixed[HEAD_DIM:, rows:]
            return attended, grad_query

        zero = jnp.zeros((HEAD_DIM, rows), jnp.float32)
        attended, grad_query = lax.fori_loop(0, pairs, grad_step, (zero, zero))
        joined = jnp.concatenate([attended, grad_query * scale], axis=0)
        odq_ref[tile] = joined.T.astype(odq_ref.dtype)
        return carry

    lax.fori_loop(0, tiles, tile_step, 0)
    scales = jnp.where(left, scale, 1.0).astype(jnp.float32)

    def near_out(at, carry):
        dnear_ref[at] = (totals[at] * scales).astype(dnear_ref.dtype)
        return carry

    def far_out(at, carry):
        dfar_ref[at] = (totals[near + at] * scales).astype(dfar_ref.dtype)
        return carry

    lax.fori_loop(0, near, near_out, 0)
    lax.fori_loop(0, far, far_out, 0)


def combine_kernel(rank_ref, near_ref, far_ref, out_ref, sums, *, ys, groups, zs, tile_dev):
    def add_near(at, carry):
        total = near_ref[0, at].astype(jnp.float32)
        for y in range(1, ys):
            total = total + near_ref[y, at].astype(jnp.float32)
        sums[at] = total
        return carry

    lax.fori_loop(0, zs * tile_dev, add_near, 0)

    def add_far(at, carry):
        rank = rank_ref[at]

        @pl.when(rank >= 0)
        def _():
            slot = (at % zs) * tile_dev + rank
            sums[slot] = sums[slot] + far_ref[at].astype(jnp.float32)

        return carry

    lax.fori_loop(0, groups * zs, add_far, 0)

    def write(at, carry):
        out_ref[at] = sums[at].astype(out_ref.dtype)
        return carry

    lax.fori_loop(0, zs * tile_dev, write, 0)


def limits(size):
    return pltpu.CompilerParams(vmem_limit_bytes=size << 20)


def vmem(count):
    return [pl.BlockSpec(memory_space=pltpu.VMEM) for _ in range(count)]


def smem(count):
    return [pl.BlockSpec(memory_space=pltpu.SMEM) for _ in range(count)]


def per_device(queries, key_input, value_input, grad_output, block_lists, block_flags):
    tile_dev = queries.shape[1]
    rows = queries.shape[3]
    width = queries.shape[4]
    entries = block_lists.shape[1]
    columns = lax.axis_size("seq")
    groups = lax.axis_size("grp")
    ys = Y_SIZE
    zs = columns // ys
    group_at = lax.axis_index("grp")
    y_at = lax.axis_index("seq") % ys
    group_tiles = tile_dev * columns
    z_groups = [[z * ys + y for z in range(zs)] for y in range(ys)]
    y_groups = [[z * ys + y for y in range(ys)] for z in range(zs)]
    bf16 = jnp.bfloat16
    near = group_tiles
    far = groups * zs
    tiles = zs * tile_dev

    lists = block_lists.reshape(groups, tile_dev, zs, ys, entries)
    flags = block_flags.reshape(groups, tile_dev, zs, ys, entries)
    lists = lax.dynamic_index_in_dim(lists, y_at, 3, keepdims=False)
    flags = lax.dynamic_index_in_dim(flags, y_at, 3, keepdims=False)
    present = lists >= 0
    safe = jnp.maximum(lists, 0)
    to_group = safe // group_tiles
    within = safe % group_tiles
    to_rank = within // columns
    to_column = within % columns
    z_ids = jnp.arange(zs, dtype=jnp.int32)[None, None, :, None]
    group_ids = jnp.arange(groups, dtype=jnp.int32)
    named = present & (to_group == group_at) & (to_column == z_ids * ys + y_at)
    far_rank = jnp.max(jnp.where(named, to_rank, -1), axis=(1, 3))
    far_rank = jnp.where(group_ids[:, None] == group_at, -1, far_rank).reshape(far)
    near_slot = (to_column % ys) * tiles + (to_column // ys) * tile_dev + to_rank
    far_slot = near + to_group * zs + z_ids
    slot = jnp.where(to_group == group_at, near_slot, far_slot)
    slot = jnp.where(present, slot, near + far)
    mask_at = jnp.where(present, jnp.where(flags != 0, 1, 0), 2)
    code = lax.dynamic_index_in_dim(slot * 4 + mask_at, group_at, 0, keepdims=False)
    code = jnp.transpose(code, (1, 0, 2)).reshape(tiles * entries)
    count = lax.dynamic_index_in_dim(present, group_at, 0, keepdims=False).astype(jnp.int32)
    count = jnp.transpose(jnp.sum(count, axis=2), (1, 0)).reshape(tiles)

    def rearrange(kernel, outs, size, *args):
        return pl.pallas_call(
            kernel, out_shape=outs, in_specs=vmem(len(args)), out_specs=vmem(len(outs)),
            compiler_params=limits(size),
        )(*args)

    head_shape = jax.ShapeDtypeStruct((HEADS, tile_dev, rows, 128), bf16)
    tile_shape = jax.ShapeDtypeStruct((tile_dev, rows, width), bf16)

    def flat(source):
        return source.reshape(tile_dev, rows, width)

    send_kv, send_qg = rearrange(
        pack_kernel, (head_shape, head_shape), 16,
        flat(queries), flat(key_input), flat(value_input), flat(grad_output),
    )

    def over_z(source):
        return lax.all_to_all(
            source, "seq", split_axis=0, concat_axis=0, tiled=True, axis_index_groups=z_groups
        )

    kv = over_z(send_kv)
    qg = over_z(send_qg)
    near_kv = lax.all_gather(
        kv.reshape(tiles, rows, 128), "seq", axis=0, tiled=True, axis_index_groups=y_groups
    )
    far_send = pl.pallas_call(
        functools.partial(far_kernel, groups=groups, zs=zs),
        out_shape=jax.ShapeDtypeStruct((far, rows, 128), bf16),
        in_specs=smem(1) + vmem(1), out_specs=vmem(1)[0], compiler_params=limits(16),
    )(far_rank, kv)
    far_kv = lax.all_to_all(far_send, "grp", split_axis=0, concat_axis=0, tiled=True)

    slots = near + far + 1
    odq, dnear, dfar = pl.pallas_call(
        functools.partial(attend_kernel, tiles=tiles, entries=entries, near=near, far=far),
        out_shape=(
            jax.ShapeDtypeStruct((tiles, rows, 128), bf16),
            jax.ShapeDtypeStruct((near, rows, 128), bf16),
            jax.ShapeDtypeStruct((far, rows, 128), bf16),
        ),
        in_specs=smem(2) + [pl.BlockSpec(memory_space=pl.ANY)] * 2 + vmem(1),
        out_specs=vmem(3),
        scratch_shapes=[
            pltpu.VMEM((slots, rows, 128), bf16),
            pltpu.VMEM((slots, rows, 128), jnp.float32),
            pltpu.VMEM((entries, rows, rows), jnp.float32),
            pltpu.VMEM((entries, rows, rows), jnp.float32),
            pltpu.VMEM((3, rows, rows), jnp.float32),
            pltpu.VMEM((2 * rows, 128), bf16),
            pltpu.SemaphoreType.DMA((2,)),
        ],
        compiler_params=limits(48),
    )(code, count, near_kv, far_kv, qg.reshape(tiles, rows, 128))

    far_back = lax.all_to_all(dfar, "grp", split_axis=0, concat_axis=0, tiled=True)
    near_back = lax.all_to_all(
        dnear, "seq", split_axis=0, concat_axis=0, tiled=True, axis_index_groups=y_groups
    )
    odq_back = over_z(odq.reshape(zs, tile_dev, rows, 128))
    dkv = pl.pallas_call(
        functools.partial(combine_kernel, ys=ys, groups=groups, zs=zs, tile_dev=tile_dev),
        out_shape=jax.ShapeDtypeStruct((tiles, rows, 128), bf16),
        in_specs=smem(1) + vmem(2), out_specs=vmem(1)[0],
        scratch_shapes=[pltpu.VMEM((tiles, rows, 128), jnp.float32)],
        compiler_params=limits(24),
    )(far_rank, near_back.reshape(ys, tiles, rows, 128), far_back)
    dkv_back = over_z(dkv.reshape(zs, tile_dev, rows, 128))
    attended, grad_queries = rearrange(unpack_kernel, (tile_shape, tile_shape), 16, odq_back)
    grad_keys, grad_values = rearrange(unpack_kernel, (tile_shape, tile_shape), 16, dkv_back)
    return tuple(
        out.reshape(1, tile_dev, 1, rows, width)
        for out in (attended, grad_queries, grad_keys, grad_values)
    )


def solution(mesh):
    spec = P("grp", None, "seq", None, None)
    return jax.shard_map(
        per_device,
        mesh=mesh,
        in_specs=(spec, spec, spec, spec, P(), P()),
        out_specs=(spec, spec, spec, spec),
        check_vma=False,
    )
```

```python
import functools

import jax
import jax.numpy as jnp
from jax import lax
from jax.experimental import pallas as pl
from jax.experimental.pallas import tpu as pltpu
from jax.sharding import PartitionSpec as P

HEADS = 8
HEAD_DIM = 64
Y_SIZE = 4
LOG2E = 1.4426950408889634
HIDDEN = -1e30


def pack_kernel(first_ref, second_ref, out_ref, first, second, packed, sems):
    copies = [
        pltpu.make_async_copy(first_ref, first, sems.at[0]),
        pltpu.make_async_copy(second_ref, second, sems.at[1]),
    ]
    for copy in copies:
        copy.start()
    for copy in copies:
        copy.wait()
    for head in range(HEADS):
        cols = slice(head * HEAD_DIM, (head + 1) * HEAD_DIM)
        packed[head] = jnp.concatenate([first[:, :, cols], second[:, :, cols]], axis=-1)
    copy = pltpu.make_async_copy(packed, out_ref, sems.at[2])
    copy.start()
    copy.wait()


def unpack_kernel(in_ref, first_ref, second_ref, packed, first, second, sems):
    copy = pltpu.make_async_copy(in_ref, packed, sems.at[2])
    copy.start()
    copy.wait()
    for pair in range(HEADS // 2):
        even = packed[2 * pair]
        odd = packed[2 * pair + 1]
        cols = slice(pair * 128, pair * 128 + 128)
        first[:, :, cols] = jnp.concatenate([even[..., :HEAD_DIM], odd[..., :HEAD_DIM]], axis=-1)
        second[:, :, cols] = jnp.concatenate([even[..., HEAD_DIM:], odd[..., HEAD_DIM:]], axis=-1)
    copies = [
        pltpu.make_async_copy(first, first_ref, sems.at[0]),
        pltpu.make_async_copy(second, second_ref, sems.at[1]),
    ]
    for copy in copies:
        copy.start()
    for copy in copies:
        copy.wait()


def far_kernel(rank_ref, kv_ref, out_ref, sem, *, far, zs, tile_dev):
    def step(at, carry):
        slot = (at % zs) * tile_dev + jnp.maximum(rank_ref[at], 0)
        pltpu.make_async_copy(kv_ref.at[slot], out_ref.at[at], sem).start()
        return carry

    lax.fori_loop(0, far, step, 0, unroll=4)
    pltpu.make_async_copy(out_ref, out_ref, sem).wait()


def attend_kernel(*refs, tiles, entries, ys, far):
    code_ref, count_ref = refs[:2]
    kv_refs = refs[2 : 3 + ys]
    qg_ref = refs[3 + ys]
    odq_ref = refs[4 + ys]
    dkv_refs = refs[5 + ys : 6 + 2 * ys]
    table, totals, scores, dprobs, masks, qg_tiles, sems = refs[6 + 2 * ys :]
    spans = [(at * tiles, tiles) for at in range(ys)] + [(ys * tiles, far)]
    slots_all = ys * tiles + far
    copies = [
        pltpu.make_async_copy(ref, table.at[pl.ds(*span)], sems.at[at])
        for at, (ref, span) in enumerate(zip(kv_refs, spans))
    ]
    copies.append(pltpu.make_async_copy(qg_ref, qg_tiles, sems.at[ys + 1]))
    for copy in copies:
        copy.start()
    rows = 128
    key_at = lax.broadcasted_iota(jnp.int32, (rows, rows), 0)
    query_at = lax.broadcasted_iota(jnp.int32, (rows, rows), 1)
    masks[0] = jnp.zeros((rows, rows), jnp.float32)
    masks[1] = jnp.where(key_at <= query_at, 0.0, HIDDEN).astype(jnp.float32)
    masks[2] = jnp.full((rows, rows), HIDDEN, jnp.float32)
    table[slots_all] = jnp.zeros((rows, rows), table.dtype)

    def clear(at, carry):
        totals[at] = jnp.zeros((rows, rows), jnp.float32)
        return carry

    lax.fori_loop(0, slots_all + 1, clear, 0, unroll=7)
    for copy in copies:
        copy.wait()
    left = query_at < HEAD_DIM
    scale = HEAD_DIM ** -0.5
    group = 4

    def fold(block, op):
        return op(block.reshape(rows // 8, 8, rows), axis=0)

    def one_tile(tile, size):
        qg = qg_tiles[tile]
        none = jnp.zeros_like(qg)
        weights = jnp.concatenate([jnp.where(left, qg, none), jnp.where(left, none, qg)], axis=0)
        codes = [code_ref[tile * entries + entry] for entry in range(size)]
        slots = [code // 4 for code in codes]
        top = jnp.full((8, rows), HIDDEN, jnp.float32)
        for start in range(0, size, group):
            kv = jnp.concatenate([table[slot] for slot in slots[start : start + group]], axis=0)
            both = lax.dot_general(
                kv, weights, (((1,), (1,)), ((), ())), preferred_element_type=jnp.float32
            )
            for at in range(group):
                entry = start + at
                part = both[at * rows : (at + 1) * rows]
                masked = part[:, :rows] + masks[codes[entry] % 4]
                scores[entry] = masked
                dprobs[entry] = part[:, rows:]
                top = jnp.maximum(top, fold(masked, jnp.max))
        row_top = jnp.max(top, axis=0, keepdims=True)
        total = jnp.zeros((8, rows), jnp.float32)
        mixed = total
        for entry in range(size):
            prob = jnp.exp2((scores[entry] - row_top) * (scale * LOG2E))
            scores[entry] = prob
            total = total + fold(prob, jnp.sum)
            mixed = mixed + fold(prob * dprobs[entry], jnp.sum)
        inverse = 1.0 / jnp.sum(total, axis=0, keepdims=True)
        delta = jnp.sum(mixed, axis=0, keepdims=True) * inverse
        attended = jnp.zeros((HEAD_DIM, rows), jnp.float32)
        grad_query = attended
        for start in range(0, size, group):
            parts = []
            for entry in range(start, start + group):
                prob = scores[entry] * inverse
                dscore = prob * (dprobs[entry] - delta)
                parts.append(jnp.concatenate([dscore, prob], axis=1).astype(jnp.bfloat16))
            both = jnp.concatenate(parts, axis=0)
            chosen = slots[start : start + group]
            added = jnp.dot(both, weights, preferred_element_type=jnp.float32)
            before = [totals[slot] for slot in chosen]
            for at in range(group):
                totals[chosen[at]] = before[at] + added[at * rows : (at + 1) * rows]
            kv = jnp.concatenate([table[slot] for slot in chosen], axis=0)
            back = lax.dot_general(
                kv, both, (((0,), (0,)), ((), ())), preferred_element_type=jnp.float32
            )
            attended = attended + back[HEAD_DIM:, rows:]
            grad_query = grad_query + back[:HEAD_DIM, :rows]
        joined = jnp.concatenate([attended, grad_query * scale], axis=0)
        qg_tiles[tile] = joined.T.astype(qg_tiles.dtype)

    def tile_step(tile, carry):
        count = count_ref[tile]
        for size in range(group, entries + 1, group):

            @pl.when((count > size - group) & (count <= size))
            def _():
                one_tile(tile, size)

        return carry

    lax.fori_loop(0, tiles, tile_step, 0)
    copies = [pltpu.make_async_copy(qg_tiles, odq_ref, sems.at[ys + 1])]
    copies[0].start()
    scales = jnp.where(left, scale, 1.0).astype(jnp.float32)

    def write(at, carry):
        table[at] = (totals[at] * scales).astype(table.dtype)
        return carry

    for at in (ys, *range(ys)):
        first, size = spans[at]
        lax.fori_loop(first, first + size, write, 0, unroll=4)
        copies.append(pltpu.make_async_copy(table.at[pl.ds(first, size)], dkv_refs[at], sems.at[at]))
        copies[-1].start()
    for copy in copies:
        copy.wait()


def combine_kernel(*refs, ys, far, zs, tile_dev):
    rank_ref = refs[0]
    near_refs = refs[1 : 1 + ys]
    far_ref, out_ref, near, far_tiles, sums, sems = refs[1 + ys :]
    tiles = zs * tile_dev
    copies = [
        pltpu.make_async_copy(ref, near.at[at], sems.at[at]) for at, ref in enumerate(near_refs)
    ]
    copies.append(pltpu.make_async_copy(far_ref, far_tiles, sems.at[ys]))
    for copy in copies:
        copy.start()
    for copy in copies:
        copy.wait()

    def add_near(at, carry):
        total = near[0, at].astype(jnp.float32)
        for y in range(1, ys):
            total = total + near[y, at].astype(jnp.float32)
        sums[at] = total
        return carry

    lax.fori_loop(0, tiles, add_near, 0, unroll=2)

    def add_far(at, carry):
        rank = rank_ref[at]

        @pl.when(rank >= 0)
        def _():
            slot = (at % zs) * tile_dev + rank
            sums[slot] = sums[slot] + far_tiles[at].astype(jnp.float32)

        return carry

    lax.fori_loop(0, far, add_far, 0)

    def write(at, carry):
        near[0, at] = sums[at].astype(near.dtype)
        return carry

    lax.fori_loop(0, tiles, write, 0, unroll=4)
    copy = pltpu.make_async_copy(near.at[0], out_ref, sems.at[0])
    copy.start()
    copy.wait()


def pin(source):
    return pltpu.with_memory_space_constraint(source, pltpu.HBM)


def limits(size):
    return pltpu.CompilerParams(vmem_limit_bytes=size << 20)


def hbm(count):
    return [pl.BlockSpec(memory_space=pl.ANY) for _ in range(count)]


def smem(count):
    return [pl.BlockSpec(memory_space=pltpu.SMEM) for _ in range(count)]


def per_device(queries, key_input, value_input, grad_output, block_lists, block_flags):
    tile_dev = queries.shape[1]
    rows = queries.shape[3]
    width = queries.shape[4]
    entries = block_lists.shape[1]
    columns = lax.axis_size("seq")
    groups = lax.axis_size("grp")
    ys = Y_SIZE
    zs = columns // ys
    group_at = lax.axis_index("grp")
    y_at = lax.axis_index("seq") % ys
    group_tiles = tile_dev * columns
    z_groups = [[z * ys + y for z in range(zs)] for y in range(ys)]
    bf16 = jnp.bfloat16
    near = group_tiles
    far = groups * zs
    tiles = zs * tile_dev

    lists = block_lists.reshape(groups, tile_dev, zs, ys, entries)
    flags = block_flags.reshape(groups, tile_dev, zs, ys, entries)
    lists = lax.dynamic_index_in_dim(lists, y_at, 3, keepdims=False)
    flags = lax.dynamic_index_in_dim(flags, y_at, 3, keepdims=False)
    present = lists >= 0
    safe = jnp.maximum(lists, 0)
    to_group = safe // group_tiles
    within = safe % group_tiles
    to_rank = within // columns
    to_column = within % columns
    z_ids = jnp.arange(zs, dtype=jnp.int32)[None, None, :, None]
    group_ids = jnp.arange(groups, dtype=jnp.int32)
    named = present & (to_group == group_at) & (to_column == z_ids * ys + y_at)
    far_rank = jnp.max(jnp.where(named, to_rank, -1), axis=(1, 3))
    far_rank = jnp.where(group_ids[:, None] == group_at, -1, far_rank).reshape(far)
    near_slot = ((to_column - y_at) % ys) * tiles + (to_column // ys) * tile_dev + to_rank
    far_slot = near + to_group * zs + z_ids
    slot = jnp.where(to_group == group_at, near_slot, far_slot)
    slot = jnp.where(present, slot, near + far)
    mask_at = jnp.where(present, jnp.where(flags != 0, 1, 0), 2)
    code = lax.dynamic_index_in_dim(slot * 4 + mask_at, group_at, 0, keepdims=False)
    code = jnp.transpose(code, (1, 0, 2)).reshape(tiles * entries)
    count = lax.dynamic_index_in_dim(present, group_at, 0, keepdims=False).astype(jnp.int32)
    count = jnp.transpose(jnp.sum(count, axis=2), (1, 0)).reshape(tiles)

    def shape_of(*shape):
        return pltpu.HBM(shape, bf16)

    head_shape = shape_of(HEADS, tile_dev, rows, 128)
    tile_shape = shape_of(tile_dev, rows, width)
    block_shape = shape_of(tiles, rows, 128)
    far_shape = shape_of(far, rows, 128)

    def scratch(shape, dtype=bf16):
        return pltpu.VMEM(shape.shape, dtype)

    def pack(first, second):
        return pl.pallas_call(
            pack_kernel,
            out_shape=head_shape,
            in_specs=hbm(2),
            out_specs=hbm(1)[0],
            scratch_shapes=[scratch(tile_shape), scratch(tile_shape), scratch(head_shape), pltpu.SemaphoreType.DMA((3,))],
            compiler_params=limits(16),
        )(pin(first.reshape(tile_shape.shape)), pin(second.reshape(tile_shape.shape)))

    def unpack(joined):
        first, second = pl.pallas_call(
            unpack_kernel,
            out_shape=(tile_shape, tile_shape),
            in_specs=hbm(1),
            out_specs=hbm(2),
            scratch_shapes=[scratch(head_shape), scratch(tile_shape), scratch(tile_shape), pltpu.SemaphoreType.DMA((3,))],
            compiler_params=limits(16),
        )(joined.reshape(head_shape.shape))
        return (
            first.reshape(1, tile_dev, 1, rows, width),
            second.reshape(1, tile_dev, 1, rows, width),
        )

    def over_z(source):
        return lax.all_to_all(
            source.reshape(head_shape.shape),
            "seq",
            split_axis=0,
            concat_axis=0,
            tiled=True,
            axis_index_groups=z_groups,
        ).reshape(block_shape.shape)

    def over_groups(source):
        return lax.all_to_all(source, "grp", split_axis=0, concat_axis=0, tiled=True)

    def over_y(source, shift):
        pairs = [(z * ys + y, z * ys + (y + shift) % ys) for z in range(zs) for y in range(ys)]
        return lax.ppermute(source, "seq", pairs)

    def after(source, *others):
        return lax.optimization_barrier((source, *others))

    kv = over_z(pack(key_input, value_input))
    send_qg = pack(queries, grad_output)
    near_kv = [kv] + [over_y(kv, -shift) for shift in range(1, ys)]
    far_send = pl.pallas_call(
        functools.partial(far_kernel, far=far, zs=zs, tile_dev=tile_dev),
        out_shape=far_shape,
        in_specs=smem(1) + hbm(1),
        out_specs=hbm(1)[0],
        scratch_shapes=[pltpu.SemaphoreType.DMA],
        compiler_params=limits(8),
    )(far_rank, kv)
    far_kv = over_groups(far_send)
    send_qg, far_kv, near_kv[1], near_kv[-1] = after(send_qg, far_kv, near_kv[1], near_kv[-1])
    qg = over_z(send_qg)

    slots = near + far + 1
    odq, *dkv_parts = pl.pallas_call(
        functools.partial(attend_kernel, tiles=tiles, entries=entries, ys=ys, far=far),
        out_shape=(block_shape,) * (ys + 1) + (far_shape,),
        in_specs=smem(2) + hbm(ys + 2),
        out_specs=hbm(ys + 2),
        scratch_shapes=[
            pltpu.VMEM((slots, rows, 128), bf16),
            pltpu.VMEM((slots, rows, 128), jnp.float32),
            pltpu.VMEM((entries, rows, rows), jnp.float32),
            pltpu.VMEM((entries, rows, rows), jnp.float32),
            pltpu.VMEM((3, rows, rows), jnp.float32),
            scratch(block_shape),
            pltpu.SemaphoreType.DMA((ys + 2,)),
        ],
        compiler_params=limits(40),
    )(code, count, kv, *map(pin, near_kv[1:]), pin(far_kv), qg)

    near_back = [dkv_parts[0]] + [over_y(dkv_parts[shift], shift) for shift in range(1, ys)]
    far_back = over_groups(dkv_parts[ys])
    odq, far_back, near_back[1], near_back[-1] = after(odq, far_back, near_back[1], near_back[-1])
    odq_back = over_z(odq)
    dkv = pl.pallas_call(
        functools.partial(combine_kernel, ys=ys, far=far, zs=zs, tile_dev=tile_dev),
        out_shape=block_shape,
        in_specs=smem(1) + hbm(ys + 1),
        out_specs=hbm(1)[0],
        scratch_shapes=[
            pltpu.VMEM((ys, tiles, rows, 128), bf16),
            scratch(far_shape),
            scratch(block_shape, jnp.float32),
            pltpu.SemaphoreType.DMA((ys + 1,)),
        ],
        compiler_params=limits(24),
    )(far_rank, *map(pin, near_back), pin(far_back))
    attended, grad_queries = unpack(odq_back)
    grad_keys, grad_values = unpack(over_z(dkv))
    return attended, grad_queries, grad_keys, grad_values


def solution(mesh):
    spec = P("grp", None, "seq", None, None)
    return jax.shard_map(
        per_device,
        mesh=mesh,
        in_specs=(spec, spec, spec, spec, P(), P()),
        out_specs=(spec, spec, spec, spec),
        check_vma=False,
    )
```

```python
import functools

import jax
import jax.numpy as jnp
from jax import lax
from jax.experimental import pallas as pl
from jax.experimental.pallas import tpu as pltpu
from jax.sharding import PartitionSpec as P

HEADS = 8
HEAD_DIM = 64
Y_SIZE = 4
LOG2E = 1.4426950408889634
HIDDEN = -1e30


def pack_kernel(first_ref, second_ref, out_ref, first, second, packed, sems):
    copies = [
        pltpu.make_async_copy(first_ref, first, sems.at[0]),
        pltpu.make_async_copy(second_ref, second, sems.at[1]),
    ]
    for copy in copies:
        copy.start()
    for copy in copies:
        copy.wait()
    for head in range(HEADS):
        cols = slice(head * HEAD_DIM, (head + 1) * HEAD_DIM)
        packed[head] = jnp.concatenate([first[:, :, cols], second[:, :, cols]], axis=-1)
    copy = pltpu.make_async_copy(packed, out_ref, sems.at[2])
    copy.start()
    copy.wait()


def pack_apart_kernel(z_ref, first_ref, second_ref, *refs):
    outs, (first, second, packed, sems) = refs[:HEADS], refs[HEADS:]
    copies = [
        pltpu.make_async_copy(first_ref, first, sems.at[0]),
        pltpu.make_async_copy(second_ref, second, sems.at[1]),
    ]
    for copy in copies:
        copy.start()
    for copy in copies:
        copy.wait()
    for head in range(HEADS):
        cols = slice(head * HEAD_DIM, (head + 1) * HEAD_DIM)
        packed[head] = jnp.concatenate([first[:, :, cols], second[:, :, cols]], axis=-1)
    copies = [
        pltpu.make_async_copy(packed.at[(z_ref[0] + shift) % HEADS], out, sems.at[shift])
        for shift, out in enumerate(outs)
    ]
    for copy in copies:
        copy.start()
    for copy in copies:
        copy.wait()


def unpack_kernel(in_ref, first_ref, second_ref, packed, first, second, sems):
    copy = pltpu.make_async_copy(in_ref, packed, sems.at[2])
    copy.start()
    copy.wait()
    unpack_heads(first_ref, second_ref, packed, first, second, sems)


def unpack_apart_kernel(z_ref, *refs):
    ins, (first_ref, second_ref, packed, first, second, sems) = refs[:HEADS], refs[HEADS:]
    copies = [
        pltpu.make_async_copy(source, packed.at[(z_ref[0] + HEADS - shift) % HEADS], sems.at[shift])
        for shift, source in enumerate(ins)
    ]
    for copy in copies:
        copy.start()
    for copy in copies:
        copy.wait()
    unpack_heads(first_ref, second_ref, packed, first, second, sems)


def unpack_heads(first_ref, second_ref, packed, first, second, sems):
    for pair in range(HEADS // 2):
        even = packed[2 * pair]
        odd = packed[2 * pair + 1]
        cols = slice(pair * 128, pair * 128 + 128)
        first[:, :, cols] = jnp.concatenate([even[..., :HEAD_DIM], odd[..., :HEAD_DIM]], axis=-1)
        second[:, :, cols] = jnp.concatenate([even[..., HEAD_DIM:], odd[..., HEAD_DIM:]], axis=-1)
    copies = [
        pltpu.make_async_copy(first, first_ref, sems.at[0]),
        pltpu.make_async_copy(second, second_ref, sems.at[1]),
    ]
    for copy in copies:
        copy.start()
    for copy in copies:
        copy.wait()


def far_kernel(rank_ref, kv_ref, out_ref, sem, *, far, zs, tile_dev):
    def step(at, carry):
        slot = (at % zs) * tile_dev + jnp.maximum(rank_ref[at], 0)
        pltpu.make_async_copy(kv_ref.at[slot], out_ref.at[at], sem).start()
        return carry

    lax.fori_loop(0, far, step, 0, unroll=4)
    pltpu.make_async_copy(out_ref, out_ref, sem).wait()


def attend_kernel(*refs, tiles, entries, ys, zs, far):
    code_ref, count_ref, z_ref = refs[:3]
    refs = refs[3:]
    kv_refs, refs = refs[: ys + 1], refs[ys + 1 :]
    qg_refs, refs = refs[:zs], refs[zs:]
    odq_refs, refs = refs[:zs], refs[zs:]
    dkv_refs, refs = refs[: ys + 1], refs[ys + 1 :]
    table, totals, scores, dprobs, masks, qg_tiles, sems = refs
    tile_dev = tiles // zs

    def z_part(distance):
        return qg_tiles.at[pl.ds(((z_ref[0] + zs + distance) % zs) * tile_dev, tile_dev)]

    spans = [(at * tiles, tiles) for at in range(ys)] + [(ys * tiles, far)]
    slots_all = ys * tiles + far
    copies = [
        pltpu.make_async_copy(ref, table.at[pl.ds(*span)], sems.at[at])
        for at, (ref, span) in enumerate(zip(kv_refs, spans))
    ]
    copies += [
        pltpu.make_async_copy(ref, z_part(-at), sems.at[ys + 1 + at])
        for at, ref in enumerate(qg_refs)
    ]
    for copy in copies:
        copy.start()
    rows = 128
    key_at = lax.broadcasted_iota(jnp.int32, (rows, rows), 0)
    query_at = lax.broadcasted_iota(jnp.int32, (rows, rows), 1)
    masks[0] = jnp.zeros((rows, rows), jnp.float32)
    masks[1] = jnp.where(key_at <= query_at, 0.0, HIDDEN).astype(jnp.float32)
    masks[2] = jnp.full((rows, rows), HIDDEN, jnp.float32)
    table[slots_all] = jnp.zeros((rows, rows), table.dtype)

    def clear(at, carry):
        totals[at] = jnp.zeros((rows, rows), jnp.float32)
        return carry

    lax.fori_loop(0, slots_all + 1, clear, 0, unroll=7)
    for copy in copies:
        copy.wait()
    left = query_at < HEAD_DIM
    scale = HEAD_DIM ** -0.5
    group = 4

    def fold(block, op):
        return op(block.reshape(rows // 8, 8, rows), axis=0)

    def one_tile(tile, size):
        qg = qg_tiles[tile]
        none = jnp.zeros_like(qg)
        weights = jnp.concatenate([jnp.where(left, qg, none), jnp.where(left, none, qg)], axis=0)
        codes = [code_ref[tile * entries + entry] for entry in range(size)]
        slots = [code // 4 for code in codes]
        top = jnp.full((8, rows), HIDDEN, jnp.float32)
        for start in range(0, size, group):
            kv = jnp.concatenate([table[slot] for slot in slots[start : start + group]], axis=0)
            both = lax.dot_general(
                kv, weights, (((1,), (1,)), ((), ())), preferred_element_type=jnp.float32
            )
            for at in range(group):
                entry = start + at
                part = both[at * rows : (at + 1) * rows]
                masked = part[:, :rows] + masks[codes[entry] % 4]
                scores[entry] = masked
                dprobs[entry] = part[:, rows:]
                top = jnp.maximum(top, fold(masked, jnp.max))
        row_top = jnp.max(top, axis=0, keepdims=True)
        total = jnp.zeros((8, rows), jnp.float32)
        mixed = total
        for entry in range(size):
            prob = jnp.exp2((scores[entry] - row_top) * (scale * LOG2E))
            scores[entry] = prob
            total = total + fold(prob, jnp.sum)
            mixed = mixed + fold(prob * dprobs[entry], jnp.sum)
        inverse = 1.0 / jnp.sum(total, axis=0, keepdims=True)
        delta = jnp.sum(mixed, axis=0, keepdims=True) * inverse
        attended = jnp.zeros((HEAD_DIM, rows), jnp.float32)
        grad_query = attended
        for start in range(0, size, group):
            parts = []
            for entry in range(start, start + group):
                prob = scores[entry] * inverse
                dscore = prob * (dprobs[entry] - delta)
                parts.append(jnp.concatenate([dscore, prob], axis=1).astype(jnp.bfloat16))
            both = jnp.concatenate(parts, axis=0)
            chosen = slots[start : start + group]
            added = jnp.dot(both, weights, preferred_element_type=jnp.float32)
            before = [totals[slot] for slot in chosen]
            for at in range(group):
                totals[chosen[at]] = before[at] + added[at * rows : (at + 1) * rows]
            kv = jnp.concatenate([table[slot] for slot in chosen], axis=0)
            back = lax.dot_general(
                kv, both, (((0,), (0,)), ((), ())), preferred_element_type=jnp.float32
            )
            attended = attended + back[HEAD_DIM:, rows:]
            grad_query = grad_query + back[:HEAD_DIM, :rows]
        joined = jnp.concatenate([attended, grad_query * scale], axis=0)
        qg_tiles[tile] = joined.T.astype(qg_tiles.dtype)

    def tile_step(tile, carry):
        count = count_ref[tile]
        for size in range(group, entries + 1, group):

            @pl.when((count > size - group) & (count <= size))
            def _():
                one_tile(tile, size)

        return carry

    lax.fori_loop(0, tiles, tile_step, 0)
    copies = [
        pltpu.make_async_copy(z_part(at), ref, sems.at[ys + 1 + at])
        for at, ref in enumerate(odq_refs)
    ]
    for copy in copies:
        copy.start()
    scales = jnp.where(left, scale, 1.0).astype(jnp.float32)

    def write(at, carry):
        table[at] = (totals[at] * scales).astype(table.dtype)
        return carry

    for at in (ys, *range(ys)):
        first, size = spans[at]
        lax.fori_loop(first, first + size, write, 0, unroll=4)
        copies.append(pltpu.make_async_copy(table.at[pl.ds(first, size)], dkv_refs[at], sems.at[at]))
        copies[-1].start()
    for copy in copies:
        copy.wait()


def combine_kernel(*refs, ys, far, zs, tile_dev):
    rank_ref = refs[0]
    near_refs = refs[1 : 1 + ys]
    far_ref, out_ref, near, far_tiles, sums, sems = refs[1 + ys :]
    tiles = zs * tile_dev
    copies = [
        pltpu.make_async_copy(ref, near.at[at], sems.at[at]) for at, ref in enumerate(near_refs)
    ]
    copies.append(pltpu.make_async_copy(far_ref, far_tiles, sems.at[ys]))
    for copy in copies:
        copy.start()
    for copy in copies:
        copy.wait()

    def add_near(at, carry):
        total = near[0, at].astype(jnp.float32)
        for y in range(1, ys):
            total = total + near[y, at].astype(jnp.float32)
        sums[at] = total
        return carry

    lax.fori_loop(0, tiles, add_near, 0, unroll=2)

    def add_far(at, carry):
        rank = rank_ref[at]

        @pl.when(rank >= 0)
        def _():
            slot = (at % zs) * tile_dev + rank
            sums[slot] = sums[slot] + far_tiles[at].astype(jnp.float32)

        return carry

    lax.fori_loop(0, far, add_far, 0)

    def write(at, carry):
        near[0, at] = sums[at].astype(near.dtype)
        return carry

    lax.fori_loop(0, tiles, write, 0, unroll=4)
    copy = pltpu.make_async_copy(near.at[0], out_ref, sems.at[0])
    copy.start()
    copy.wait()


def pin(source):
    return pltpu.with_memory_space_constraint(source, pltpu.HBM)


def limits(size):
    return pltpu.CompilerParams(vmem_limit_bytes=size << 20)


def hbm(count):
    return [pl.BlockSpec(memory_space=pl.ANY) for _ in range(count)]


def smem(count):
    return [pl.BlockSpec(memory_space=pltpu.SMEM) for _ in range(count)]


def per_device(queries, key_input, value_input, grad_output, block_lists, block_flags):
    tile_dev = queries.shape[1]
    rows = queries.shape[3]
    width = queries.shape[4]
    entries = block_lists.shape[1]
    columns = lax.axis_size("seq")
    groups = lax.axis_size("grp")
    ys = Y_SIZE
    zs = columns // ys
    group_at = lax.axis_index("grp")
    y_at = lax.axis_index("seq") % ys
    group_tiles = tile_dev * columns
    z_groups = [[z * ys + y for z in range(zs)] for y in range(ys)]
    bf16 = jnp.bfloat16
    near = group_tiles
    far = groups * zs
    tiles = zs * tile_dev

    lists = block_lists.reshape(groups, tile_dev, zs, ys, entries)
    flags = block_flags.reshape(groups, tile_dev, zs, ys, entries)
    lists = lax.dynamic_index_in_dim(lists, y_at, 3, keepdims=False)
    flags = lax.dynamic_index_in_dim(flags, y_at, 3, keepdims=False)
    present = lists >= 0
    safe = jnp.maximum(lists, 0)
    to_group = safe // group_tiles
    within = safe % group_tiles
    to_rank = within // columns
    to_column = within % columns
    z_ids = jnp.arange(zs, dtype=jnp.int32)[None, None, :, None]
    group_ids = jnp.arange(groups, dtype=jnp.int32)
    named = present & (to_group == group_at) & (to_column == z_ids * ys + y_at)
    far_rank = jnp.max(jnp.where(named, to_rank, -1), axis=(1, 3))
    far_rank = jnp.where(group_ids[:, None] == group_at, -1, far_rank).reshape(far)
    near_slot = ((to_column - y_at) % ys) * tiles + (to_column // ys) * tile_dev + to_rank
    far_slot = near + to_group * zs + z_ids
    slot = jnp.where(to_group == group_at, near_slot, far_slot)
    slot = jnp.where(present, slot, near + far)
    mask_at = jnp.where(present, jnp.where(flags != 0, 1, 0), 2)
    code = lax.dynamic_index_in_dim(slot * 4 + mask_at, group_at, 0, keepdims=False)
    code = jnp.transpose(code, (1, 0, 2)).reshape(tiles * entries)
    count = lax.dynamic_index_in_dim(present, group_at, 0, keepdims=False).astype(jnp.int32)
    count = jnp.transpose(jnp.sum(count, axis=2), (1, 0)).reshape(tiles)

    def shape_of(*shape):
        return pltpu.HBM(shape, bf16)

    head_shape = shape_of(HEADS, tile_dev, rows, 128)
    tile_shape = shape_of(tile_dev, rows, width)
    block_shape = shape_of(tiles, rows, 128)
    far_shape = shape_of(far, rows, 128)

    def scratch(shape, dtype=bf16):
        return pltpu.VMEM(shape.shape, dtype)

    def pack(first, second):
        return pl.pallas_call(
            pack_kernel,
            out_shape=head_shape,
            in_specs=hbm(2),
            out_specs=hbm(1)[0],
            scratch_shapes=[scratch(tile_shape), scratch(tile_shape), scratch(head_shape), pltpu.SemaphoreType.DMA((3,))],
            compiler_params=limits(16),
        )(pin(first.reshape(tile_shape.shape)), pin(second.reshape(tile_shape.shape)))

    z_at = jnp.reshape(lax.axis_index("seq") // ys, (1,)).astype(jnp.int32)
    part_shape = shape_of(tile_dev, rows, 128)

    def pack_apart(first, second):
        return pl.pallas_call(
            pack_apart_kernel,
            out_shape=(part_shape,) * zs,
            in_specs=smem(1) + hbm(2),
            out_specs=hbm(zs),
            scratch_shapes=[scratch(tile_shape), scratch(tile_shape), scratch(head_shape), pltpu.SemaphoreType.DMA((zs,))],
            compiler_params=limits(16),
        )(z_at, pin(first.reshape(tile_shape.shape)), pin(second.reshape(tile_shape.shape)))

    def unpack_apart(parts):
        first, second = pl.pallas_call(
            unpack_apart_kernel,
            out_shape=(tile_shape, tile_shape),
            in_specs=smem(1) + hbm(zs),
            out_specs=hbm(2),
            scratch_shapes=[scratch(head_shape), scratch(tile_shape), scratch(tile_shape), pltpu.SemaphoreType.DMA((zs,))],
            compiler_params=limits(16),
        )(z_at, *map(pin, parts))
        return (
            first.reshape(1, tile_dev, 1, rows, width),
            second.reshape(1, tile_dev, 1, rows, width),
        )

    def shift_z(source, shift):
        pairs = [(z * ys + y, ((z + shift) % zs) * ys + y) for z in range(zs) for y in range(ys)]
        return lax.ppermute(source, "seq", pairs)

    def unpack(joined):
        first, second = pl.pallas_call(
            unpack_kernel,
            out_shape=(tile_shape, tile_shape),
            in_specs=hbm(1),
            out_specs=hbm(2),
            scratch_shapes=[scratch(head_shape), scratch(tile_shape), scratch(tile_shape), pltpu.SemaphoreType.DMA((3,))],
            compiler_params=limits(16),
        )(joined.reshape(head_shape.shape))
        return (
            first.reshape(1, tile_dev, 1, rows, width),
            second.reshape(1, tile_dev, 1, rows, width),
        )

    def over_z(source):
        return lax.all_to_all(
            source.reshape(head_shape.shape),
            "seq",
            split_axis=0,
            concat_axis=0,
            tiled=True,
            axis_index_groups=z_groups,
        ).reshape(block_shape.shape)

    def over_groups(source):
        return lax.all_to_all(source, "grp", split_axis=0, concat_axis=0, tiled=True)

    def over_y(source, shift):
        pairs = [(z * ys + y, z * ys + (y + shift) % ys) for z in range(zs) for y in range(ys)]
        return lax.ppermute(source, "seq", pairs)

    kv = over_z(pack(key_input, value_input))
    qg = list(pack_apart(queries, grad_output))
    near_kv = [kv] + [over_y(kv, -shift) for shift in range(1, ys)]
    far_send = pl.pallas_call(
        functools.partial(far_kernel, far=far, zs=zs, tile_dev=tile_dev),
        out_shape=far_shape,
        in_specs=smem(1) + hbm(1),
        out_specs=hbm(1)[0],
        scratch_shapes=[pltpu.SemaphoreType.DMA],
        compiler_params=limits(8),
    )(far_rank, kv)
    far_kv = over_groups(far_send)
    qg[1:] = [shift_z(qg[shift], shift) for shift in range(1, zs)]

    slots = near + far + 1
    parts = pl.pallas_call(
        functools.partial(attend_kernel, tiles=tiles, entries=entries, ys=ys, zs=zs, far=far),
        out_shape=(part_shape,) * zs + (block_shape,) * ys + (far_shape,),
        in_specs=smem(3) + hbm(ys + 1 + zs),
        out_specs=hbm(ys + 1 + zs),
        scratch_shapes=[
            pltpu.VMEM((slots, rows, 128), bf16),
            pltpu.VMEM((slots, rows, 128), jnp.float32),
            pltpu.VMEM((entries, rows, rows), jnp.float32),
            pltpu.VMEM((entries, rows, rows), jnp.float32),
            pltpu.VMEM((3, rows, rows), jnp.float32),
            scratch(block_shape),
            pltpu.SemaphoreType.DMA((ys + 1 + zs,)),
        ],
        compiler_params=limits(40),
    )(code, count, z_at, kv, *map(pin, near_kv[1:]), far_kv, *map(pin, qg))
    odq, dkv_parts = list(parts[:zs]), parts[zs:]

    near_back = [dkv_parts[0]] + [over_y(dkv_parts[shift], shift) for shift in range(1, ys)]
    far_back = over_groups(dkv_parts[ys])
    odq[1:] = [shift_z(odq[shift], shift) for shift in range(1, zs)]
    last_rank, *odq[1:] = lax.optimization_barrier((far_rank, *odq[1:]))
    dkv = pl.pallas_call(
        functools.partial(combine_kernel, ys=ys, far=far, zs=zs, tile_dev=tile_dev),
        out_shape=block_shape,
        in_specs=smem(1) + hbm(ys + 1),
        out_specs=hbm(1)[0],
        scratch_shapes=[
            pltpu.VMEM((ys, tiles, rows, 128), bf16),
            scratch(far_shape),
            scratch(block_shape, jnp.float32),
            pltpu.SemaphoreType.DMA((ys + 1,)),
        ],
        compiler_params=limits(24),
    )(last_rank, *map(pin, near_back), far_back)
    attended, grad_queries = unpack_apart(odq)
    grad_keys, grad_values = unpack(over_z(dkv))
    return attended, grad_queries, grad_keys, grad_values


def solution(mesh):
    spec = P("grp", None, "seq", None, None)
    return jax.shard_map(
        per_device,
        mesh=mesh,
        in_specs=(spec, spec, spec, spec, P(), P()),
        out_specs=(spec, spec, spec, spec),
        check_vma=False,
    )
```

```python
import functools

import jax
import jax.numpy as jnp
from jax import lax
from jax.experimental import pallas as pl
from jax.experimental.pallas import tpu as pltpu
from jax.sharding import PartitionSpec as P

HEADS = 8
HEAD_DIM = 64
Y_SIZE = 4
LOG2E = 1.4426950408889634
HIDDEN = -1e30


def pack_kernel(first_ref, second_ref, out_ref, first, second, packed, sems):
    copies = [
        pltpu.make_async_copy(first_ref, first, sems.at[0]),
        pltpu.make_async_copy(second_ref, second, sems.at[1]),
    ]
    for copy in copies:
        copy.start()
    for copy in copies:
        copy.wait()
    for head in range(HEADS):
        cols = slice(head * HEAD_DIM, (head + 1) * HEAD_DIM)
        packed[head] = jnp.concatenate([first[:, :, cols], second[:, :, cols]], axis=-1)
    copy = pltpu.make_async_copy(packed, out_ref, sems.at[2])
    copy.start()
    copy.wait()


def pack_apart_kernel(z_ref, first_ref, second_ref, *refs):
    outs, (first, second, packed, sems) = refs[:HEADS], refs[HEADS:]
    copies = [
        pltpu.make_async_copy(first_ref, first, sems.at[0]),
        pltpu.make_async_copy(second_ref, second, sems.at[1]),
    ]
    for copy in copies:
        copy.start()
    for copy in copies:
        copy.wait()
    for head in range(HEADS):
        cols = slice(head * HEAD_DIM, (head + 1) * HEAD_DIM)
        packed[head] = jnp.concatenate([first[:, :, cols], second[:, :, cols]], axis=-1)
    copies = [
        pltpu.make_async_copy(packed.at[(z_ref[0] + shift) % HEADS], out, sems.at[shift])
        for shift, out in enumerate(outs)
    ]
    for copy in copies:
        copy.start()
    for copy in copies:
        copy.wait()


def unpack_kernel(in_ref, first_ref, second_ref, packed, first, second, sems):
    copy = pltpu.make_async_copy(in_ref, packed, sems.at[2])
    copy.start()
    copy.wait()
    unpack_heads(first_ref, second_ref, packed, first, second, sems)


def unpack_apart_kernel(z_ref, *refs):
    ins, (first_ref, second_ref, packed, first, second, sems) = refs[:HEADS], refs[HEADS:]
    copies = [
        pltpu.make_async_copy(source, packed.at[(z_ref[0] + HEADS - shift) % HEADS], sems.at[shift])
        for shift, source in enumerate(ins)
    ]
    for copy in copies:
        copy.start()
    for copy in copies:
        copy.wait()
    unpack_heads(first_ref, second_ref, packed, first, second, sems)


def unpack_heads(first_ref, second_ref, packed, first, second, sems):
    for pair in range(HEADS // 2):
        even = packed[2 * pair]
        odd = packed[2 * pair + 1]
        cols = slice(pair * 128, pair * 128 + 128)
        first[:, :, cols] = jnp.concatenate([even[..., :HEAD_DIM], odd[..., :HEAD_DIM]], axis=-1)
        second[:, :, cols] = jnp.concatenate([even[..., HEAD_DIM:], odd[..., HEAD_DIM:]], axis=-1)
    copies = [
        pltpu.make_async_copy(first, first_ref, sems.at[0]),
        pltpu.make_async_copy(second, second_ref, sems.at[1]),
    ]
    for copy in copies:
        copy.start()
    for copy in copies:
        copy.wait()


def far_kernel(rank_ref, kv_ref, out_ref, sem, *, far, zs, tile_dev):
    def step(at, carry):
        slot = (at % zs) * tile_dev + jnp.maximum(rank_ref[at], 0)
        pltpu.make_async_copy(kv_ref.at[slot], out_ref.at[at], sem).start()
        return carry

    lax.fori_loop(0, far, step, 0, unroll=4)
    pltpu.make_async_copy(out_ref, out_ref, sem).wait()


def attend_kernel(*refs, tiles, entries, ys, zs, far):
    code_ref, count_ref, z_ref = refs[:3]
    refs = refs[3:]
    kv_refs, refs = refs[: ys + 1], refs[ys + 1 :]
    qg_refs, refs = refs[:zs], refs[zs:]
    odq_refs, refs = refs[:zs], refs[zs:]
    dkv_refs, refs = refs[: ys + 1], refs[ys + 1 :]
    table, totals, scores, dprobs, masks, qg_tiles, sems = refs
    tile_dev = tiles // zs

    def z_part(distance):
        return qg_tiles.at[pl.ds(((z_ref[0] + zs + distance) % zs) * tile_dev, tile_dev)]

    spans = [(at * tiles, tiles) for at in range(ys)] + [(ys * tiles, far)]
    slots_all = ys * tiles + far
    copies = [
        pltpu.make_async_copy(ref, table.at[pl.ds(*span)], sems.at[at])
        for at, (ref, span) in enumerate(zip(kv_refs, spans))
    ]
    copies += [
        pltpu.make_async_copy(ref, z_part(-at), sems.at[ys + 1 + at])
        for at, ref in enumerate(qg_refs)
    ]
    for copy in copies:
        copy.start()
    rows = 128
    key_at = lax.broadcasted_iota(jnp.int32, (rows, rows), 0)
    query_at = lax.broadcasted_iota(jnp.int32, (rows, rows), 1)
    masks[0] = jnp.zeros((rows, rows), jnp.float32)
    masks[1] = jnp.where(key_at <= query_at, 0.0, HIDDEN).astype(jnp.float32)
    masks[2] = jnp.full((rows, rows), HIDDEN, jnp.float32)
    table[slots_all] = jnp.zeros((rows, rows), table.dtype)

    def clear(at, carry):
        totals[at] = jnp.zeros((rows, rows), jnp.float32)
        return carry

    lax.fori_loop(0, slots_all + 1, clear, 0, unroll=7)
    for copy in copies:
        copy.wait()
    left = query_at < HEAD_DIM
    scale = HEAD_DIM ** -0.5
    group = 4
    banks = 3
    chain = 4

    def fold(block, op):
        return op(block.reshape(rows // 8, 8, rows), axis=0)

    class Tile:
        def __init__(self, tile, size, bank):
            self.tile = tile
            self.first = bank * entries
            qg = qg_tiles[tile]
            none = jnp.zeros_like(qg)
            self.weights = jnp.concatenate([jnp.where(left, qg, none), jnp.where(left, none, qg)], axis=0)
            self.codes = [code_ref[tile * entries + entry] for entry in range(size)]
            self.slots = [code // 4 for code in self.codes]
            self.top = jnp.full((8, rows), HIDDEN, jnp.float32)
            self.total = jnp.zeros((8, rows), jnp.float32)
            self.mixed = self.total
            self.attended = jnp.zeros((HEAD_DIM, rows), jnp.float32)
            self.grad_query = self.attended

        def score(self, start):
            kv = jnp.concatenate([table[slot] for slot in self.slots[start : start + group]], axis=0)
            both = lax.dot_general(
                kv, self.weights, (((1,), (1,)), ((), ())), preferred_element_type=jnp.float32
            )
            for at in range(group):
                entry = start + at
                part = both[at * rows : (at + 1) * rows]
                masked = part[:, :rows] + masks[self.codes[entry] % 4]
                scores[self.first + entry] = masked
                dprobs[self.first + entry] = part[:, rows:]
                self.top = jnp.maximum(self.top, fold(masked, jnp.max))

        def score_end(self):
            self.row_top = jnp.max(self.top, axis=0, keepdims=True)

        def exp(self, start):
            for entry in range(self.first + start, self.first + start + group):
                prob = jnp.exp2((scores[entry] - self.row_top) * (scale * LOG2E))
                scores[entry] = prob
                self.total = self.total + fold(prob, jnp.sum)
                self.mixed = self.mixed + fold(prob * dprobs[entry], jnp.sum)

        def exp_end(self):
            self.inverse = 1.0 / jnp.sum(self.total, axis=0, keepdims=True)
            self.delta = jnp.sum(self.mixed, axis=0, keepdims=True) * self.inverse

        def grad(self, start):
            parts = []
            for entry in range(self.first + start, self.first + start + group):
                prob = scores[entry] * self.inverse
                dscore = prob * (dprobs[entry] - self.delta)
                parts.append(jnp.concatenate([dscore, prob], axis=1).astype(jnp.bfloat16))
            both = jnp.concatenate(parts, axis=0)
            chosen = self.slots[start : start + group]
            added = jnp.dot(both, self.weights, preferred_element_type=jnp.float32)
            before = [totals[slot] for slot in chosen]
            for at in range(group):
                totals[chosen[at]] = before[at] + added[at * rows : (at + 1) * rows]
            kv = jnp.concatenate([table[slot] for slot in chosen], axis=0)
            back = lax.dot_general(
                kv, both, (((0,), (0,)), ((), ())), preferred_element_type=jnp.float32
            )
            self.attended = self.attended + back[HEAD_DIM:, rows:]
            self.grad_query = self.grad_query + back[:HEAD_DIM, :rows]

        def grad_end(self):
            joined = jnp.concatenate([self.attended, self.grad_query * scale], axis=0)
            qg_tiles[self.tile] = joined.T.astype(qg_tiles.dtype)

    def run_chain(ids, size):
        live = []
        for at in range(len(ids) + 2):
            if at < len(ids):
                live.append(Tile(ids[at], size, at % banks))
            ready = [live[at - back] if 0 <= at - back < len(ids) else None for back in range(3)]
            for start in range(0, size, group):
                if ready[2]:
                    ready[2].grad(start)
                if ready[1]:
                    ready[1].exp(start)
                if ready[0]:
                    ready[0].score(start)
            if ready[2]:
                ready[2].grad_end()
            if ready[1]:
                ready[1].exp_end()
            if ready[0]:
                ready[0].score_end()

    def chain_step(step, carry):
        first = (step // tile_dev) * chain * tile_dev + step % tile_dev
        ids = [first + at * tile_dev for at in range(chain)]
        count = count_ref[ids[0]]
        for tile in ids[1:]:
            count = jnp.maximum(count, count_ref[tile])
        for size in range(group, entries + 1, group):

            @pl.when((count > size - group) & (count <= size))
            def _():
                run_chain(ids, size)

        return carry

    lax.fori_loop(0, tiles // chain, chain_step, 0)
    copies = [
        pltpu.make_async_copy(z_part(at), ref, sems.at[ys + 1 + at])
        for at, ref in enumerate(odq_refs)
    ]
    for copy in copies:
        copy.start()
    scales = jnp.where(left, scale, 1.0).astype(jnp.float32)

    def write(at, carry):
        table[at] = (totals[at] * scales).astype(table.dtype)
        return carry

    for at in (ys, *range(ys)):
        first, size = spans[at]
        lax.fori_loop(first, first + size, write, 0, unroll=4)
        copies.append(pltpu.make_async_copy(table.at[pl.ds(first, size)], dkv_refs[at], sems.at[at]))
        copies[-1].start()
    for copy in copies:
        copy.wait()


def combine_kernel(*refs, ys, groups, zs, tile_dev):
    rank_ref = refs[0]
    near_refs = refs[1 : 1 + ys]
    far_ref, out_ref, near, far_tiles, sums, sems = refs[1 + ys :]
    halves = 2
    span = zs // halves
    copies = []
    for half in range(halves):
        part = pl.ds(half * span * tile_dev, span * tile_dev)
        copies.append(
            [
                pltpu.make_async_copy(ref.at[part], near.at[at, part], sems.at[half, at])
                for at, ref in enumerate(near_refs)
            ]
            + [
                pltpu.make_async_copy(
                    far_ref.at[:, pl.ds(half * span, span)],
                    far_tiles.at[:, pl.ds(half * span, span)],
                    sems.at[half, ys],
                )
            ]
        )
    for batch in copies:
        for copy in batch:
            copy.start()

    def z_step(z, carry):
        first = z * tile_dev
        for rank in range(tile_dev):
            total = near[0, first + rank].astype(jnp.float32)
            for y in range(1, ys):
                total = total + near[y, first + rank].astype(jnp.float32)
            sums[first + rank] = total
        for group in range(groups):
            rank = rank_ref[group * zs + z]

            @pl.when(rank >= 0)
            def _():
                sums[first + rank] = sums[first + rank] + far_tiles[group, z].astype(jnp.float32)

        for rank in range(tile_dev):
            near[0, first + rank] = sums[first + rank].astype(near.dtype)
        return carry

    outs = []
    for half in range(halves):
        for copy in copies[half]:
            copy.wait()
        lax.fori_loop(half * span, (half + 1) * span, z_step, 0)
        part = pl.ds(half * span * tile_dev, span * tile_dev)
        outs.append(pltpu.make_async_copy(near.at[0, part], out_ref.at[part], sems.at[half, ys + 1]))
        outs[-1].start()
    for copy in outs:
        copy.wait()


def pin(source):
    return pltpu.with_memory_space_constraint(source, pltpu.HBM)


def limits(size):
    return pltpu.CompilerParams(vmem_limit_bytes=size << 20)


def hbm(count):
    return [pl.BlockSpec(memory_space=pl.ANY) for _ in range(count)]


def smem(count):
    return [pl.BlockSpec(memory_space=pltpu.SMEM) for _ in range(count)]


def per_device(queries, key_input, value_input, grad_output, block_lists, block_flags):
    tile_dev = queries.shape[1]
    rows = queries.shape[3]
    width = queries.shape[4]
    entries = block_lists.shape[1]
    columns = lax.axis_size("seq")
    groups = lax.axis_size("grp")
    ys = Y_SIZE
    zs = columns // ys
    group_at = lax.axis_index("grp")
    y_at = lax.axis_index("seq") % ys
    group_tiles = tile_dev * columns
    z_groups = [[z * ys + y for z in range(zs)] for y in range(ys)]
    bf16 = jnp.bfloat16
    near = group_tiles
    far = groups * zs
    tiles = zs * tile_dev

    lists = block_lists.reshape(groups, tile_dev, zs, ys, entries)
    flags = block_flags.reshape(groups, tile_dev, zs, ys, entries)
    lists = lax.dynamic_index_in_dim(lists, y_at, 3, keepdims=False)
    flags = lax.dynamic_index_in_dim(flags, y_at, 3, keepdims=False)
    present = lists >= 0
    safe = jnp.maximum(lists, 0)
    to_group = safe // group_tiles
    within = safe % group_tiles
    to_rank = within // columns
    to_column = within % columns
    z_ids = jnp.arange(zs, dtype=jnp.int32)[None, None, :, None]
    group_ids = jnp.arange(groups, dtype=jnp.int32)
    named = present & (to_group == group_at) & (to_column == z_ids * ys + y_at)
    far_rank = jnp.max(jnp.where(named, to_rank, -1), axis=(1, 3))
    far_rank = jnp.where(group_ids[:, None] == group_at, -1, far_rank).reshape(far)
    near_slot = ((to_column - y_at) % ys) * tiles + (to_column // ys) * tile_dev + to_rank
    far_slot = near + to_group * zs + z_ids
    slot = jnp.where(to_group == group_at, near_slot, far_slot)
    slot = jnp.where(present, slot, near + far)
    mask_at = jnp.where(present, jnp.where(flags != 0, 1, 0), 2)
    code = lax.dynamic_index_in_dim(slot * 4 + mask_at, group_at, 0, keepdims=False)
    code = jnp.transpose(code, (1, 0, 2)).reshape(tiles * entries)
    count = lax.dynamic_index_in_dim(present, group_at, 0, keepdims=False).astype(jnp.int32)
    count = jnp.transpose(jnp.sum(count, axis=2), (1, 0)).reshape(tiles)

    def shape_of(*shape):
        return pltpu.HBM(shape, bf16)

    head_shape = shape_of(HEADS, tile_dev, rows, 128)
    tile_shape = shape_of(tile_dev, rows, width)
    block_shape = shape_of(tiles, rows, 128)
    far_shape = shape_of(far, rows, 128)

    def scratch(shape, dtype=bf16):
        return pltpu.VMEM(shape.shape, dtype)

    def pack(first, second):
        return pl.pallas_call(
            pack_kernel,
            out_shape=head_shape,
            in_specs=hbm(2),
            out_specs=hbm(1)[0],
            scratch_shapes=[scratch(tile_shape), scratch(tile_shape), scratch(head_shape), pltpu.SemaphoreType.DMA((3,))],
            compiler_params=limits(16),
        )(pin(first.reshape(tile_shape.shape)), pin(second.reshape(tile_shape.shape)))

    z_at = jnp.reshape(lax.axis_index("seq") // ys, (1,)).astype(jnp.int32)
    part_shape = shape_of(tile_dev, rows, 128)

    def pack_apart(first, second):
        return pl.pallas_call(
            pack_apart_kernel,
            out_shape=(part_shape,) * zs,
            in_specs=smem(1) + hbm(2),
            out_specs=hbm(zs),
            scratch_shapes=[scratch(tile_shape), scratch(tile_shape), scratch(head_shape), pltpu.SemaphoreType.DMA((zs,))],
            compiler_params=limits(16),
        )(z_at, pin(first.reshape(tile_shape.shape)), pin(second.reshape(tile_shape.shape)))

    def unpack_apart(parts):
        first, second = pl.pallas_call(
            unpack_apart_kernel,
            out_shape=(tile_shape, tile_shape),
            in_specs=smem(1) + hbm(zs),
            out_specs=hbm(2),
            scratch_shapes=[scratch(head_shape), scratch(tile_shape), scratch(tile_shape), pltpu.SemaphoreType.DMA((zs,))],
            compiler_params=limits(16),
        )(z_at, *map(pin, parts))
        return (
            first.reshape(1, tile_dev, 1, rows, width),
            second.reshape(1, tile_dev, 1, rows, width),
        )

    def shift_z(source, shift):
        pairs = [(z * ys + y, ((z + shift) % zs) * ys + y) for z in range(zs) for y in range(ys)]
        return lax.ppermute(source, "seq", pairs)

    def unpack(joined):
        first, second = pl.pallas_call(
            unpack_kernel,
            out_shape=(tile_shape, tile_shape),
            in_specs=hbm(1),
            out_specs=hbm(2),
            scratch_shapes=[scratch(head_shape), scratch(tile_shape), scratch(tile_shape), pltpu.SemaphoreType.DMA((3,))],
            compiler_params=limits(16),
        )(joined.reshape(head_shape.shape))
        return (
            first.reshape(1, tile_dev, 1, rows, width),
            second.reshape(1, tile_dev, 1, rows, width),
        )

    def over_z(source):
        return lax.all_to_all(
            source.reshape(head_shape.shape),
            "seq",
            split_axis=0,
            concat_axis=0,
            tiled=True,
            axis_index_groups=z_groups,
        ).reshape(block_shape.shape)

    def over_groups(source):
        return lax.all_to_all(source, "grp", split_axis=0, concat_axis=0, tiled=True)

    def over_y(source, shift):
        pairs = [(z * ys + y, z * ys + (y + shift) % ys) for z in range(zs) for y in range(ys)]
        return lax.ppermute(source, "seq", pairs)

    kv = over_z(pack(key_input, value_input))
    qg = list(pack_apart(queries, grad_output))
    near_kv = [kv] + [over_y(kv, -shift) for shift in range(1, ys)]
    far_send = pl.pallas_call(
        functools.partial(far_kernel, far=far, zs=zs, tile_dev=tile_dev),
        out_shape=far_shape,
        in_specs=smem(1) + hbm(1),
        out_specs=hbm(1)[0],
        scratch_shapes=[pltpu.SemaphoreType.DMA],
        compiler_params=limits(8),
    )(far_rank, kv)
    far_kv = over_groups(far_send)
    qg[1:] = [shift_z(qg[shift], shift) for shift in range(1, zs)]

    slots = near + far + 1
    parts = pl.pallas_call(
        functools.partial(attend_kernel, tiles=tiles, entries=entries, ys=ys, zs=zs, far=far),
        out_shape=(part_shape,) * zs + (block_shape,) * ys + (far_shape,),
        in_specs=smem(3) + hbm(ys + 1 + zs),
        out_specs=hbm(ys + 1 + zs),
        scratch_shapes=[
            pltpu.VMEM((slots, rows, 128), bf16),
            pltpu.VMEM((slots, rows, 128), jnp.float32),
            pltpu.VMEM((3 * entries, rows, rows), jnp.float32),
            pltpu.VMEM((3 * entries, rows, rows), jnp.float32),
            pltpu.VMEM((3, rows, rows), jnp.float32),
            scratch(block_shape),
            pltpu.SemaphoreType.DMA((ys + 1 + zs,)),
        ],
        compiler_params=limits(48),
    )(code, count, z_at, kv, *map(pin, near_kv[1:]), far_kv, *map(pin, qg))
    odq, dkv_parts = list(parts[:zs]), parts[zs:]

    near_back = [dkv_parts[0]] + [over_y(dkv_parts[shift], shift) for shift in range(1, ys)]
    far_back = over_groups(dkv_parts[ys])
    odq[1:] = [shift_z(odq[shift], shift) for shift in range(1, zs)]
    last_rank, *odq[1:] = lax.optimization_barrier((far_rank, *odq[1:]))
    dkv = pl.pallas_call(
        functools.partial(combine_kernel, ys=ys, groups=groups, zs=zs, tile_dev=tile_dev),
        out_shape=block_shape,
        in_specs=smem(1) + hbm(ys + 1),
        out_specs=hbm(1)[0],
        scratch_shapes=[
            pltpu.VMEM((ys, tiles, rows, 128), bf16),
            pltpu.VMEM((groups, zs, rows, 128), bf16),
            scratch(block_shape, jnp.float32),
            pltpu.SemaphoreType.DMA((2, ys + 2)),
        ],
        compiler_params=limits(24),
    )(last_rank, *map(pin, near_back), far_back.reshape(groups, zs, rows, 128))
    attended, grad_queries = unpack_apart(odq)
    grad_keys, grad_values = unpack(over_z(dkv))
    return attended, grad_queries, grad_keys, grad_values


def solution(mesh):
    spec = P("grp", None, "seq", None, None)
    return jax.shard_map(
        per_device,
        mesh=mesh,
        in_specs=(spec, spec, spec, spec, P(), P()),
        out_specs=(spec, spec, spec, spec),
        check_vma=False,
    )
```

```python
import functools

import jax
import jax.numpy as jnp
from jax import lax
from jax.experimental import pallas as pl
from jax.experimental.pallas import tpu as pltpu
from jax.sharding import PartitionSpec as P

HEADS = 8
HEAD_DIM = 64
Y_SIZE = 4
LOG2E = 1.4426950408889634
HIDDEN = -1e30


def pack_kernel(first_ref, second_ref, out_ref, first, second, packed, sems):
    copies = [
        pltpu.make_async_copy(first_ref, first, sems.at[0]),
        pltpu.make_async_copy(second_ref, second, sems.at[1]),
    ]
    for copy in copies:
        copy.start()
    for copy in copies:
        copy.wait()
    for head in range(HEADS):
        cols = slice(head * HEAD_DIM, (head + 1) * HEAD_DIM)
        packed[head] = jnp.concatenate([first[:, :, cols], second[:, :, cols]], axis=-1)
    copy = pltpu.make_async_copy(packed, out_ref, sems.at[2])
    copy.start()
    copy.wait()


def pack_apart_kernel(z_ref, first_ref, second_ref, *refs):
    outs, (first, second, packed, sems) = refs[:HEADS], refs[HEADS:]
    copies = [
        pltpu.make_async_copy(first_ref, first, sems.at[0]),
        pltpu.make_async_copy(second_ref, second, sems.at[1]),
    ]
    for copy in copies:
        copy.start()
    for copy in copies:
        copy.wait()
    for head in range(HEADS):
        cols = slice(head * HEAD_DIM, (head + 1) * HEAD_DIM)
        packed[head] = jnp.concatenate([first[:, :, cols], second[:, :, cols]], axis=-1)
    copies = [
        pltpu.make_async_copy(packed.at[(z_ref[0] + shift) % HEADS], out, sems.at[shift])
        for shift, out in enumerate(outs)
    ]
    for copy in copies:
        copy.start()
    for copy in copies:
        copy.wait()


def unpack_kernel(in_ref, first_ref, second_ref, packed, first, second, sems):
    copy = pltpu.make_async_copy(in_ref, packed, sems.at[2])
    copy.start()
    copy.wait()
    unpack_heads(first_ref, second_ref, packed, first, second, sems)


def unpack_apart_kernel(z_ref, *refs):
    ins, (first_ref, second_ref, packed, first, second, sems) = refs[:HEADS], refs[HEADS:]
    copies = [
        pltpu.make_async_copy(source, packed.at[(z_ref[0] + HEADS - shift) % HEADS], sems.at[shift])
        for shift, source in enumerate(ins)
    ]
    for copy in copies:
        copy.start()
    for copy in copies:
        copy.wait()
    unpack_heads(first_ref, second_ref, packed, first, second, sems)


def unpack_heads(first_ref, second_ref, packed, first, second, sems):
    for pair in range(HEADS // 2):
        even = packed[2 * pair]
        odd = packed[2 * pair + 1]
        cols = slice(pair * 128, pair * 128 + 128)
        first[:, :, cols] = jnp.concatenate([even[..., :HEAD_DIM], odd[..., :HEAD_DIM]], axis=-1)
        second[:, :, cols] = jnp.concatenate([even[..., HEAD_DIM:], odd[..., HEAD_DIM:]], axis=-1)
    copies = [
        pltpu.make_async_copy(first, first_ref, sems.at[0]),
        pltpu.make_async_copy(second, second_ref, sems.at[1]),
    ]
    for copy in copies:
        copy.start()
    for copy in copies:
        copy.wait()


def far_kernel(rank_ref, kv_ref, out_ref, sem, *, far, zs, tile_dev):
    def step(at, carry):
        slot = (at % zs) * tile_dev + jnp.maximum(rank_ref[at], 0)
        pltpu.make_async_copy(kv_ref.at[slot], out_ref.at[at], sem).start()
        return carry

    lax.fori_loop(0, far, step, 0, unroll=4)
    pltpu.make_async_copy(out_ref, out_ref, sem).wait()


def attend_kernel(*refs, tiles, entries, ys, zs, far):
    code_ref, count_ref, z_ref = refs[:3]
    refs = refs[3:]
    kv_refs, refs = refs[: ys + 1], refs[ys + 1 :]
    qg_refs, refs = refs[:zs], refs[zs:]
    odq_refs, refs = refs[:zs], refs[zs:]
    dkv_refs, refs = refs[: ys + 1], refs[ys + 1 :]
    table, totals, scores, dprobs, masks, qg_tiles, sems = refs
    tile_dev = tiles // zs

    def z_part(distance):
        return qg_tiles.at[pl.ds(((z_ref[0] + zs + distance) % zs) * tile_dev, tile_dev)]

    spans = [(at * tiles, tiles) for at in range(ys)] + [(ys * tiles, far)]
    slots_all = ys * tiles + far
    copies = [
        pltpu.make_async_copy(ref, table.at[pl.ds(*span)], sems.at[at])
        for at, (ref, span) in enumerate(zip(kv_refs, spans))
    ]
    copies += [
        pltpu.make_async_copy(ref, z_part(-at), sems.at[ys + 1 + at])
        for at, ref in enumerate(qg_refs)
    ]
    for copy in copies:
        copy.start()
    rows = 128
    key_at = lax.broadcasted_iota(jnp.int32, (rows, rows), 0)
    query_at = lax.broadcasted_iota(jnp.int32, (rows, rows), 1)
    masks[0] = jnp.zeros((rows, rows), jnp.float32)
    masks[1] = jnp.where(key_at <= query_at, 0.0, HIDDEN).astype(jnp.float32)
    masks[2] = jnp.full((rows, rows), HIDDEN, jnp.float32)
    table[slots_all] = jnp.zeros((rows, rows), table.dtype)

    def clear(at, carry):
        totals[at] = jnp.zeros((rows, rows), jnp.float32)
        return carry

    lax.fori_loop(0, slots_all + 1, clear, 0, unroll=7)
    for copy in copies:
        copy.wait()
    left = query_at < HEAD_DIM
    scale = HEAD_DIM ** -0.5
    group = 4
    banks = 3
    chain = 4

    def fold(block, op):
        return op(block.reshape(rows // 8, 8, rows), axis=0)

    class Tile:
        def __init__(self, tile, size, bank):
            self.tile = tile
            self.first = bank * entries
            qg = qg_tiles[tile]
            none = jnp.zeros_like(qg)
            self.weights = jnp.concatenate([jnp.where(left, qg, none), jnp.where(left, none, qg)], axis=0)
            self.codes = [code_ref[tile * entries + entry] for entry in range(size)]
            self.slots = [code // 4 for code in self.codes]
            self.top = jnp.full((8, rows), HIDDEN, jnp.float32)
            self.total = jnp.zeros((8, rows), jnp.float32)
            self.mixed = self.total
            self.attended = jnp.zeros((HEAD_DIM, rows), jnp.float32)
            self.grad_query = self.attended

        def score(self, start):
            kv = jnp.concatenate([table[slot] for slot in self.slots[start : start + group]], axis=0)
            both = lax.dot_general(
                kv, self.weights, (((1,), (1,)), ((), ())), preferred_element_type=jnp.float32
            )
            for at in range(group):
                entry = start + at
                part = both[at * rows : (at + 1) * rows]
                masked = part[:, :rows] + masks[self.codes[entry] % 4]
                scores[self.first + entry] = masked
                dprobs[self.first + entry] = part[:, rows:]
                self.top = jnp.maximum(self.top, fold(masked, jnp.max))

        def score_end(self):
            self.row_top = jnp.max(self.top, axis=0, keepdims=True)

        def exp(self, start):
            for entry in range(self.first + start, self.first + start + group):
                prob = jnp.exp2((scores[entry] - self.row_top) * (scale * LOG2E))
                scores[entry] = prob
                self.total = self.total + fold(prob, jnp.sum)
                self.mixed = self.mixed + fold(prob * dprobs[entry], jnp.sum)

        def exp_end(self):
            self.inverse = 1.0 / jnp.sum(self.total, axis=0, keepdims=True)
            self.delta = jnp.sum(self.mixed, axis=0, keepdims=True) * self.inverse

        def grad(self, start):
            parts = []
            for entry in range(self.first + start, self.first + start + group):
                prob = scores[entry] * self.inverse
                dscore = prob * (dprobs[entry] - self.delta)
                parts.append(jnp.concatenate([dscore, prob], axis=1).astype(jnp.bfloat16))
            both = jnp.concatenate(parts, axis=0)
            chosen = self.slots[start : start + group]
            added = jnp.dot(both, self.weights, preferred_element_type=jnp.float32)
            before = [totals[slot] for slot in chosen]
            for at in range(group):
                totals[chosen[at]] = before[at] + added[at * rows : (at + 1) * rows]
            kv = jnp.concatenate([table[slot] for slot in chosen], axis=0)
            back = lax.dot_general(
                kv, both, (((0,), (0,)), ((), ())), preferred_element_type=jnp.float32
            )
            self.attended = self.attended + back[HEAD_DIM:, rows:]
            self.grad_query = self.grad_query + back[:HEAD_DIM, :rows]

        def grad_end(self):
            joined = jnp.concatenate([self.attended, self.grad_query * scale], axis=0)
            qg_tiles[self.tile] = joined.T.astype(qg_tiles.dtype)

    def run_chain(ids, size):
        live = []
        for at in range(len(ids) + 2):
            if at < len(ids):
                live.append(Tile(ids[at], size, at % banks))
            ready = [live[at - back] if 0 <= at - back < len(ids) else None for back in range(3)]
            for start in range(0, size, group):
                if ready[2]:
                    ready[2].grad(start)
                if ready[1]:
                    ready[1].exp(start)
                if ready[0]:
                    ready[0].score(start)
            if ready[2]:
                ready[2].grad_end()
            if ready[1]:
                ready[1].exp_end()
            if ready[0]:
                ready[0].score_end()

    def chain_step(step, carry):
        first = (step // tile_dev) * chain * tile_dev + step % tile_dev
        ids = [first + at * tile_dev for at in range(chain)]
        count = count_ref[ids[0]]
        for tile in ids[1:]:
            count = jnp.maximum(count, count_ref[tile])
        for size in range(group, entries + 1, group):

            @pl.when((count > size - group) & (count <= size))
            def _():
                run_chain(ids, size)

        return carry

    lax.fori_loop(0, tiles // chain, chain_step, 0)
    copies = [
        pltpu.make_async_copy(z_part(at), ref, sems.at[ys + 1 + at])
        for at, ref in enumerate(odq_refs)
    ]
    for copy in copies:
        copy.start()
    scales = jnp.where(left, scale, 1.0).astype(jnp.float32)

    def write(at, carry):
        table[at] = (totals[at] * scales).astype(table.dtype)
        return carry

    for at in (ys, *range(ys)):
        first, size = spans[at]
        lax.fori_loop(first, first + size, write, 0, unroll=4)
        copies.append(pltpu.make_async_copy(table.at[pl.ds(first, size)], dkv_refs[at], sems.at[at]))
        copies[-1].start()
    for copy in copies:
        copy.wait()


def combine_kernel(*refs, ys, groups, zs, tile_dev):
    rank_ref = refs[0]
    near_refs = refs[1 : 1 + ys]
    far_ref, out_ref, near, far_tiles, sums, sems = refs[1 + ys :]
    halves = 2
    span = zs // halves
    copies = []
    for half in range(halves):
        part = pl.ds(half * span * tile_dev, span * tile_dev)
        copies.append(
            [
                pltpu.make_async_copy(ref.at[part], near.at[at, part], sems.at[half, at])
                for at, ref in enumerate(near_refs)
            ]
            + [
                pltpu.make_async_copy(
                    far_ref.at[:, pl.ds(half * span, span)],
                    far_tiles.at[:, pl.ds(half * span, span)],
                    sems.at[half, ys],
                )
            ]
        )
    for batch in copies:
        for copy in batch:
            copy.start()

    def z_step(z, carry):
        first = z * tile_dev
        for rank in range(tile_dev):
            total = near[0, first + rank].astype(jnp.float32)
            for y in range(1, ys):
                total = total + near[y, first + rank].astype(jnp.float32)
            sums[first + rank] = total
        for group in range(groups):
            rank = rank_ref[group * zs + z]

            @pl.when(rank >= 0)
            def _():
                sums[first + rank] = sums[first + rank] + far_tiles[group, z].astype(jnp.float32)

        for rank in range(tile_dev):
            near[0, first + rank] = sums[first + rank].astype(near.dtype)
        return carry

    outs = []
    for half in range(halves):
        for copy in copies[half]:
            copy.wait()
        lax.fori_loop(half * span, (half + 1) * span, z_step, 0)
        part = pl.ds(half * span * tile_dev, span * tile_dev)
        outs.append(pltpu.make_async_copy(near.at[0, part], out_ref.at[part], sems.at[half, ys + 1]))
        outs[-1].start()
    for copy in outs:
        copy.wait()


def pin(source):
    return pltpu.with_memory_space_constraint(source, pltpu.HBM)


def limits(size):
    return pltpu.CompilerParams(vmem_limit_bytes=size << 20)


def hbm(count):
    return [pl.BlockSpec(memory_space=pl.ANY) for _ in range(count)]


def smem(count):
    return [pl.BlockSpec(memory_space=pltpu.SMEM) for _ in range(count)]


def per_device(queries, key_input, value_input, grad_output, block_lists, block_flags):
    tile_dev = queries.shape[1]
    rows = queries.shape[3]
    width = queries.shape[4]
    entries = block_lists.shape[1]
    columns = lax.axis_size("seq")
    groups = lax.axis_size("grp")
    ys = Y_SIZE
    zs = columns // ys
    group_at = lax.axis_index("grp")
    y_at = lax.axis_index("seq") % ys
    group_tiles = tile_dev * columns
    z_groups = [[z * ys + y for z in range(zs)] for y in range(ys)]
    bf16 = jnp.bfloat16
    near = group_tiles
    far = groups * zs
    tiles = zs * tile_dev

    lists = block_lists.reshape(groups, tile_dev, zs, ys, entries)
    flags = block_flags.reshape(groups, tile_dev, zs, ys, entries)
    lists = lax.dynamic_index_in_dim(lists, y_at, 3, keepdims=False)
    flags = lax.dynamic_index_in_dim(flags, y_at, 3, keepdims=False)
    present = lists >= 0
    safe = jnp.maximum(lists, 0)
    to_group = safe // group_tiles
    within = safe % group_tiles
    to_rank = within // columns
    to_column = within % columns
    z_ids = jnp.arange(zs, dtype=jnp.int32)[None, None, :, None]
    group_ids = jnp.arange(groups, dtype=jnp.int32)
    named = present & (to_group == group_at) & (to_column == z_ids * ys + y_at)
    far_rank = jnp.max(jnp.where(named, to_rank, -1), axis=(1, 3))
    far_rank = jnp.where(group_ids[:, None] == group_at, -1, far_rank).reshape(far)
    near_slot = ((to_column - y_at) % ys) * tiles + (to_column // ys) * tile_dev + to_rank
    far_slot = near + to_group * zs + z_ids
    slot = jnp.where(to_group == group_at, near_slot, far_slot)
    slot = jnp.where(present, slot, near + far)
    mask_at = jnp.where(present, jnp.where(flags != 0, 1, 0), 2)
    code = lax.dynamic_index_in_dim(slot * 4 + mask_at, group_at, 0, keepdims=False)
    code = jnp.transpose(code, (1, 0, 2)).reshape(tiles * entries)
    count = lax.dynamic_index_in_dim(present, group_at, 0, keepdims=False).astype(jnp.int32)
    count = jnp.transpose(jnp.sum(count, axis=2), (1, 0)).reshape(tiles)

    def shape_of(*shape):
        return pltpu.HBM(shape, bf16)

    head_shape = shape_of(HEADS, tile_dev, rows, 128)
    tile_shape = shape_of(tile_dev, rows, width)
    block_shape = shape_of(tiles, rows, 128)
    far_shape = shape_of(far, rows, 128)

    def scratch(shape, dtype=bf16):
        return pltpu.VMEM(shape.shape, dtype)

    def pack(first, second):
        return pl.pallas_call(
            pack_kernel,
            out_shape=head_shape,
            in_specs=hbm(2),
            out_specs=hbm(1)[0],
            scratch_shapes=[scratch(tile_shape), scratch(tile_shape), scratch(head_shape), pltpu.SemaphoreType.DMA((3,))],
            compiler_params=limits(16),
        )(pin(first.reshape(tile_shape.shape)), pin(second.reshape(tile_shape.shape)))

    z_at = jnp.reshape(lax.axis_index("seq") // ys, (1,)).astype(jnp.int32)
    part_shape = shape_of(tile_dev, rows, 128)

    def pack_apart(first, second):
        return pl.pallas_call(
            pack_apart_kernel,
            out_shape=(part_shape,) * zs,
            in_specs=smem(1) + hbm(2),
            out_specs=hbm(zs),
            scratch_shapes=[scratch(tile_shape), scratch(tile_shape), scratch(head_shape), pltpu.SemaphoreType.DMA((zs,))],
            compiler_params=limits(16),
        )(z_at, pin(first.reshape(tile_shape.shape)), pin(second.reshape(tile_shape.shape)))

    def unpack_apart(parts):
        first, second = pl.pallas_call(
            unpack_apart_kernel,
            out_shape=(tile_shape, tile_shape),
            in_specs=smem(1) + hbm(zs),
            out_specs=hbm(2),
            scratch_shapes=[scratch(head_shape), scratch(tile_shape), scratch(tile_shape), pltpu.SemaphoreType.DMA((zs,))],
            compiler_params=limits(16),
        )(z_at, *map(pin, parts))
        return (
            first.reshape(1, tile_dev, 1, rows, width),
            second.reshape(1, tile_dev, 1, rows, width),
        )

    def shift_z(source, shift):
        pairs = [(z * ys + y, ((z + shift) % zs) * ys + y) for z in range(zs) for y in range(ys)]
        return lax.ppermute(source, "seq", pairs)

    def unpack(joined):
        first, second = pl.pallas_call(
            unpack_kernel,
            out_shape=(tile_shape, tile_shape),
            in_specs=hbm(1),
            out_specs=hbm(2),
            scratch_shapes=[scratch(head_shape), scratch(tile_shape), scratch(tile_shape), pltpu.SemaphoreType.DMA((3,))],
            compiler_params=limits(16),
        )(joined.reshape(head_shape.shape))
        return (
            first.reshape(1, tile_dev, 1, rows, width),
            second.reshape(1, tile_dev, 1, rows, width),
        )

    def over_z(source):
        return lax.all_to_all(
            source.reshape(head_shape.shape),
            "seq",
            split_axis=0,
            concat_axis=0,
            tiled=True,
            axis_index_groups=z_groups,
        ).reshape(block_shape.shape)

    def over_groups(source):
        return lax.all_to_all(source, "grp", split_axis=0, concat_axis=0, tiled=True)

    def over_y(source, shift):
        pairs = [(z * ys + y, z * ys + (y + shift) % ys) for z in range(zs) for y in range(ys)]
        return lax.ppermute(source, "seq", pairs)

    kv = over_z(pack(key_input, value_input))
    qg = list(pack_apart(queries, grad_output))
    first_rank, *qg = lax.optimization_barrier((far_rank, *qg))
    near_kv = [kv] + [over_y(kv, -shift) for shift in range(1, ys)]
    far_send = pl.pallas_call(
        functools.partial(far_kernel, far=far, zs=zs, tile_dev=tile_dev),
        out_shape=far_shape,
        in_specs=smem(1) + hbm(1),
        out_specs=hbm(1)[0],
        scratch_shapes=[pltpu.SemaphoreType.DMA],
        compiler_params=limits(8),
    )(first_rank, kv)
    far_kv = over_groups(far_send)
    qg[1:] = [shift_z(qg[shift], shift) for shift in range(1, zs)]

    slots = near + far + 1
    parts = pl.pallas_call(
        functools.partial(attend_kernel, tiles=tiles, entries=entries, ys=ys, zs=zs, far=far),
        out_shape=(part_shape,) * zs + (block_shape,) * ys + (far_shape,),
        in_specs=smem(3) + hbm(ys + 1 + zs),
        out_specs=hbm(ys + 1 + zs),
        scratch_shapes=[
            pltpu.VMEM((slots, rows, 128), bf16),
            pltpu.VMEM((slots, rows, 128), jnp.float32),
            pltpu.VMEM((3 * entries, rows, rows), jnp.float32),
            pltpu.VMEM((3 * entries, rows, rows), jnp.float32),
            pltpu.VMEM((3, rows, rows), jnp.float32),
            scratch(block_shape),
            pltpu.SemaphoreType.DMA((ys + 1 + zs,)),
        ],
        compiler_params=limits(48),
    )(code, count, z_at, kv, *map(pin, near_kv[1:]), far_kv, *map(pin, qg))
    odq, dkv_parts = list(parts[:zs]), parts[zs:]

    near_back = [dkv_parts[0]] + [over_y(dkv_parts[shift], shift) for shift in range(1, ys)]
    far_back = over_groups(dkv_parts[ys])
    odq[1:] = [shift_z(odq[shift], shift) for shift in range(1, zs)]
    last_rank, *odq[1:] = lax.optimization_barrier((far_rank, *odq[1:]))
    dkv = pl.pallas_call(
        functools.partial(combine_kernel, ys=ys, groups=groups, zs=zs, tile_dev=tile_dev),
        out_shape=block_shape,
        in_specs=smem(1) + hbm(ys + 1),
        out_specs=hbm(1)[0],
        scratch_shapes=[
            pltpu.VMEM((ys, tiles, rows, 128), bf16),
            pltpu.VMEM((groups, zs, rows, 128), bf16),
            scratch(block_shape, jnp.float32),
            pltpu.SemaphoreType.DMA((2, ys + 2)),
        ],
        compiler_params=limits(24),
    )(last_rank, *map(pin, near_back), far_back.reshape(groups, zs, rows, 128))
    attended, grad_queries = unpack_apart(odq)
    grad_keys, grad_values = unpack(over_z(dkv))
    return attended, grad_queries, grad_keys, grad_values


def solution(mesh):
    spec = P("grp", None, "seq", None, None)
    return jax.shard_map(
        per_device,
        mesh=mesh,
        in_specs=(spec, spec, spec, spec, P(), P()),
        out_specs=(spec, spec, spec, spec),
        check_vma=False,
    )
```

```python
import functools

import jax
import jax.numpy as jnp
from jax import lax
from jax.experimental import pallas as pl
from jax.experimental.pallas import tpu as pltpu
from jax.sharding import PartitionSpec as P

HEADS = 8
HEAD_DIM = 64
Y_SIZE = 4
LOG2E = 1.4426950408889634
HIDDEN = -1e30


def pack_kernel(first_ref, second_ref, out_ref, first, second, packed, sems):
    copies = [
        pltpu.make_async_copy(first_ref, first, sems.at[0]),
        pltpu.make_async_copy(second_ref, second, sems.at[1]),
    ]
    for copy in copies:
        copy.start()
    for copy in copies:
        copy.wait()
    for head in range(HEADS):
        cols = slice(head * HEAD_DIM, (head + 1) * HEAD_DIM)
        packed[head] = jnp.concatenate([first[:, :, cols], second[:, :, cols]], axis=-1)
    copy = pltpu.make_async_copy(packed, out_ref, sems.at[2])
    copy.start()
    copy.wait()


def pack_apart_kernel(z_ref, first_ref, second_ref, *refs):
    outs, (first, second, packed, sems) = refs[:HEADS], refs[HEADS:]
    copies = [
        pltpu.make_async_copy(first_ref, first, sems.at[0]),
        pltpu.make_async_copy(second_ref, second, sems.at[1]),
    ]
    for copy in copies:
        copy.start()
    for copy in copies:
        copy.wait()
    for head in range(HEADS):
        cols = slice(head * HEAD_DIM, (head + 1) * HEAD_DIM)
        packed[head] = jnp.concatenate([first[:, :, cols], second[:, :, cols]], axis=-1)
    copies = [
        pltpu.make_async_copy(packed.at[(z_ref[0] + shift) % HEADS], out, sems.at[shift])
        for shift, out in enumerate(outs)
    ]
    for copy in copies:
        copy.start()
    for copy in copies:
        copy.wait()


def unpack_kernel(in_ref, first_ref, second_ref, packed, first, second, sems):
    copy = pltpu.make_async_copy(in_ref, packed, sems.at[2])
    copy.start()
    copy.wait()
    unpack_heads(first_ref, second_ref, packed, first, second, sems)


def unpack_apart_kernel(z_ref, *refs):
    ins, (first_ref, second_ref, packed, first, second, sems) = refs[:HEADS], refs[HEADS:]
    copies = [
        pltpu.make_async_copy(source, packed.at[(z_ref[0] + HEADS - shift) % HEADS], sems.at[shift])
        for shift, source in enumerate(ins)
    ]
    for copy in copies:
        copy.start()
    for copy in copies:
        copy.wait()
    unpack_heads(first_ref, second_ref, packed, first, second, sems)


def unpack_heads(first_ref, second_ref, packed, first, second, sems):
    for pair in range(HEADS // 2):
        even = packed[2 * pair]
        odd = packed[2 * pair + 1]
        cols = slice(pair * 128, pair * 128 + 128)
        first[:, :, cols] = jnp.concatenate([even[..., :HEAD_DIM], odd[..., :HEAD_DIM]], axis=-1)
        second[:, :, cols] = jnp.concatenate([even[..., HEAD_DIM:], odd[..., HEAD_DIM:]], axis=-1)
    copies = [
        pltpu.make_async_copy(first, first_ref, sems.at[0]),
        pltpu.make_async_copy(second, second_ref, sems.at[1]),
    ]
    for copy in copies:
        copy.start()
    for copy in copies:
        copy.wait()


def far_kernel(rank_ref, kv_ref, out_ref, sem, *, far, zs, tile_dev):
    def step(at, carry):
        slot = (at % zs) * tile_dev + jnp.maximum(rank_ref[at], 0)
        pltpu.make_async_copy(kv_ref.at[slot], out_ref.at[at], sem).start()
        return carry

    lax.fori_loop(0, far, step, 0, unroll=4)
    pltpu.make_async_copy(out_ref, out_ref, sem).wait()


def attend_kernel(*refs, tiles, entries, ys, zs, far):
    code_ref, count_ref, z_ref = refs[:3]
    refs = refs[3:]
    kv_refs, refs = refs[: ys + 1], refs[ys + 1 :]
    qg_refs, refs = refs[:zs], refs[zs:]
    odq_refs, refs = refs[:zs], refs[zs:]
    dkv_refs, refs = refs[: ys + 1], refs[ys + 1 :]
    table, totals, scores, dprobs, masks, qg_tiles, sems = refs
    tile_dev = tiles // zs

    def z_part(distance):
        return qg_tiles.at[pl.ds(((z_ref[0] + zs + distance) % zs) * tile_dev, tile_dev)]

    spans = [(at * tiles, tiles) for at in range(ys)] + [(ys * tiles, far)]
    slots_all = ys * tiles + far
    copies = [
        pltpu.make_async_copy(ref, table.at[pl.ds(*span)], sems.at[at])
        for at, (ref, span) in enumerate(zip(kv_refs, spans))
    ]
    copies += [
        pltpu.make_async_copy(ref, z_part(-at), sems.at[ys + 1 + at])
        for at, ref in enumerate(qg_refs)
    ]
    for copy in copies:
        copy.start()
    rows = 128
    key_at = lax.broadcasted_iota(jnp.int32, (rows, rows), 0)
    query_at = lax.broadcasted_iota(jnp.int32, (rows, rows), 1)
    masks[0] = jnp.zeros((rows, rows), jnp.float32)
    masks[1] = jnp.where(key_at <= query_at, 0.0, HIDDEN).astype(jnp.float32)
    masks[2] = jnp.full((rows, rows), HIDDEN, jnp.float32)
    table[slots_all] = jnp.zeros((rows, rows), table.dtype)

    def clear(at, carry):
        totals[at] = jnp.zeros((rows, rows), jnp.float32)
        return carry

    lax.fori_loop(0, slots_all + 1, clear, 0, unroll=7)
    for copy in copies:
        copy.wait()
    left = query_at < HEAD_DIM
    scale = HEAD_DIM ** -0.5
    group = 2
    banks = 3
    chain = 4

    def fold(block, op):
        return op(block.reshape(rows // 8, 8, rows), axis=0)

    class Tile:
        def __init__(self, tile, size, bank):
            self.tile = tile
            self.first = bank * entries
            qg = qg_tiles[tile]
            none = jnp.zeros_like(qg)
            self.weights = jnp.concatenate([jnp.where(left, qg, none), jnp.where(left, none, qg)], axis=0)
            self.codes = [code_ref[tile * entries + entry] for entry in range(size)]
            self.slots = [code // 4 for code in self.codes]
            self.top = jnp.full((8, rows), HIDDEN, jnp.float32)
            self.total = jnp.zeros((8, rows), jnp.float32)
            self.mixed = self.total
            self.attended = jnp.zeros((HEAD_DIM, rows), jnp.float32)
            self.grad_query = self.attended

        def score(self, start):
            kv = jnp.concatenate([table[slot] for slot in self.slots[start : start + group]], axis=0)
            both = lax.dot_general(
                kv, self.weights, (((1,), (1,)), ((), ())), preferred_element_type=jnp.float32
            )
            for at in range(group):
                entry = start + at
                part = both[at * rows : (at + 1) * rows]
                masked = part[:, :rows] + masks[self.codes[entry] % 4]
                scores[self.first + entry] = masked
                dprobs[self.first + entry] = part[:, rows:]
                self.top = jnp.maximum(self.top, fold(masked, jnp.max))

        def score_end(self):
            self.row_top = jnp.max(self.top, axis=0, keepdims=True)

        def exp(self, start):
            for entry in range(self.first + start, self.first + start + group):
                prob = jnp.exp2((scores[entry] - self.row_top) * (scale * LOG2E))
                scores[entry] = prob
                self.total = self.total + fold(prob, jnp.sum)
                self.mixed = self.mixed + fold(prob * dprobs[entry], jnp.sum)

        def exp_end(self):
            self.inverse = 1.0 / jnp.sum(self.total, axis=0, keepdims=True)
            self.delta = jnp.sum(self.mixed, axis=0, keepdims=True) * self.inverse

        def grad(self, start):
            parts = []
            for entry in range(self.first + start, self.first + start + group):
                prob = scores[entry] * self.inverse
                dscore = prob * (dprobs[entry] - self.delta)
                parts.append(jnp.concatenate([dscore, prob], axis=1).astype(jnp.bfloat16))
            both = jnp.concatenate(parts, axis=0)
            chosen = self.slots[start : start + group]
            added = jnp.dot(both, self.weights, preferred_element_type=jnp.float32)
            before = [totals[slot] for slot in chosen]
            for at in range(group):
                totals[chosen[at]] = before[at] + added[at * rows : (at + 1) * rows]
            kv = jnp.concatenate([table[slot] for slot in chosen], axis=0)
            back = lax.dot_general(
                kv, both, (((0,), (0,)), ((), ())), preferred_element_type=jnp.float32
            )
            self.attended = self.attended + back[HEAD_DIM:, rows:]
            self.grad_query = self.grad_query + back[:HEAD_DIM, :rows]

        def grad_end(self):
            joined = jnp.concatenate([self.attended, self.grad_query * scale], axis=0)
            qg_tiles[self.tile] = joined.T.astype(qg_tiles.dtype)

    def run_chain(ids, size):
        live = []
        for at in range(len(ids) + 2):
            if at < len(ids):
                live.append(Tile(ids[at], size, at % banks))
            ready = [live[at - back] if 0 <= at - back < len(ids) else None for back in range(3)]
            for start in range(0, size, group):
                if ready[2]:
                    ready[2].grad(start)
                if ready[1]:
                    ready[1].exp(start)
                if ready[0]:
                    ready[0].score(start)
            if ready[2]:
                ready[2].grad_end()
            if ready[1]:
                ready[1].exp_end()
            if ready[0]:
                ready[0].score_end()

    def chain_step(step, carry):
        first = (step // tile_dev) * chain * tile_dev + step % tile_dev
        ids = [first + at * tile_dev for at in range(chain)]
        count = count_ref[ids[0]]
        for tile in ids[1:]:
            count = jnp.maximum(count, count_ref[tile])
        sizes = [size for size in range(group, entries + 1, group) if size >= entries // 2]
        for below, size in zip([0, *sizes], sizes):

            @pl.when((count > below) & (count <= size))
            def _():
                run_chain(ids, size)

        return carry

    lax.fori_loop(0, tiles // chain, chain_step, 0)
    copies = [
        pltpu.make_async_copy(z_part(at), ref, sems.at[ys + 1 + at])
        for at, ref in enumerate(odq_refs)
    ]
    for copy in copies:
        copy.start()
    scales = jnp.where(left, scale, 1.0).astype(jnp.float32)

    def write(at, carry):
        table[at] = (totals[at] * scales).astype(table.dtype)
        return carry

    for at in (ys, *range(ys)):
        first, size = spans[at]
        lax.fori_loop(first, first + size, write, 0, unroll=4)
        copies.append(pltpu.make_async_copy(table.at[pl.ds(first, size)], dkv_refs[at], sems.at[at]))
        copies[-1].start()
    for copy in copies:
        copy.wait()


def combine_kernel(*refs, ys, groups, zs, tile_dev):
    rank_ref = refs[0]
    near_refs = refs[1 : 1 + ys]
    far_ref, out_ref, near, far_tiles, sums, sems = refs[1 + ys :]
    halves = 2
    span = zs // halves
    copies = []
    for half in range(halves):
        part = pl.ds(half * span * tile_dev, span * tile_dev)
        copies.append(
            [
                pltpu.make_async_copy(ref.at[part], near.at[at, part], sems.at[half, at])
                for at, ref in enumerate(near_refs)
            ]
            + [
                pltpu.make_async_copy(
                    far_ref.at[:, pl.ds(half * span, span)],
                    far_tiles.at[:, pl.ds(half * span, span)],
                    sems.at[half, ys],
                )
            ]
        )
    for batch in copies:
        for copy in batch:
            copy.start()

    def z_step(z, carry):
        first = z * tile_dev
        for rank in range(tile_dev):
            total = near[0, first + rank].astype(jnp.float32)
            for y in range(1, ys):
                total = total + near[y, first + rank].astype(jnp.float32)
            sums[first + rank] = total
        for group in range(groups):
            rank = rank_ref[group * zs + z]

            @pl.when(rank >= 0)
            def _():
                sums[first + rank] = sums[first + rank] + far_tiles[group, z].astype(jnp.float32)

        for rank in range(tile_dev):
            near[0, first + rank] = sums[first + rank].astype(near.dtype)
        return carry

    outs = []
    for half in range(halves):
        for copy in copies[half]:
            copy.wait()
        lax.fori_loop(half * span, (half + 1) * span, z_step, 0)
        part = pl.ds(half * span * tile_dev, span * tile_dev)
        outs.append(pltpu.make_async_copy(near.at[0, part], out_ref.at[part], sems.at[half, ys + 1]))
        outs[-1].start()
    for copy in outs:
        copy.wait()


def pin(source):
    return pltpu.with_memory_space_constraint(source, pltpu.HBM)


def limits(size):
    return pltpu.CompilerParams(vmem_limit_bytes=size << 20)


def hbm(count):
    return [pl.BlockSpec(memory_space=pl.ANY) for _ in range(count)]


def smem(count):
    return [pl.BlockSpec(memory_space=pltpu.SMEM) for _ in range(count)]


def per_device(queries, key_input, value_input, grad_output, block_lists, block_flags):
    tile_dev = queries.shape[1]
    rows = queries.shape[3]
    width = queries.shape[4]
    entries = block_lists.shape[1]
    columns = lax.axis_size("seq")
    groups = lax.axis_size("grp")
    ys = Y_SIZE
    zs = columns // ys
    group_at = lax.axis_index("grp")
    y_at = lax.axis_index("seq") % ys
    group_tiles = tile_dev * columns
    z_groups = [[z * ys + y for z in range(zs)] for y in range(ys)]
    bf16 = jnp.bfloat16
    near = group_tiles
    far = groups * zs
    tiles = zs * tile_dev

    lists = block_lists.reshape(groups, tile_dev, zs, ys, entries)
    flags = block_flags.reshape(groups, tile_dev, zs, ys, entries)
    lists = lax.dynamic_index_in_dim(lists, y_at, 3, keepdims=False)
    flags = lax.dynamic_index_in_dim(flags, y_at, 3, keepdims=False)
    present = lists >= 0
    safe = jnp.maximum(lists, 0)
    to_group = safe // group_tiles
    within = safe % group_tiles
    to_rank = within // columns
    to_column = within % columns
    z_ids = jnp.arange(zs, dtype=jnp.int32)[None, None, :, None]
    group_ids = jnp.arange(groups, dtype=jnp.int32)
    named = present & (to_group == group_at) & (to_column == z_ids * ys + y_at)
    far_rank = jnp.max(jnp.where(named, to_rank, -1), axis=(1, 3))
    far_rank = jnp.where(group_ids[:, None] == group_at, -1, far_rank).reshape(far)
    near_slot = ((to_column - y_at) % ys) * tiles + (to_column // ys) * tile_dev + to_rank
    far_slot = near + to_group * zs + z_ids
    slot = jnp.where(to_group == group_at, near_slot, far_slot)
    slot = jnp.where(present, slot, near + far)
    mask_at = jnp.where(present, jnp.where(flags != 0, 1, 0), 2)
    code = lax.dynamic_index_in_dim(slot * 4 + mask_at, group_at, 0, keepdims=False)
    code = jnp.transpose(code, (1, 0, 2)).reshape(tiles * entries)
    count = lax.dynamic_index_in_dim(present, group_at, 0, keepdims=False).astype(jnp.int32)
    count = jnp.transpose(jnp.sum(count, axis=2), (1, 0)).reshape(tiles)

    def shape_of(*shape):
        return pltpu.HBM(shape, bf16)

    head_shape = shape_of(HEADS, tile_dev, rows, 128)
    tile_shape = shape_of(tile_dev, rows, width)
    block_shape = shape_of(tiles, rows, 128)
    far_shape = shape_of(far, rows, 128)

    def scratch(shape, dtype=bf16):
        return pltpu.VMEM(shape.shape, dtype)

    def pack(first, second):
        return pl.pallas_call(
            pack_kernel,
            out_shape=head_shape,
            in_specs=hbm(2),
            out_specs=hbm(1)[0],
            scratch_shapes=[scratch(tile_shape), scratch(tile_shape), scratch(head_shape), pltpu.SemaphoreType.DMA((3,))],
            compiler_params=limits(16),
        )(pin(first.reshape(tile_shape.shape)), pin(second.reshape(tile_shape.shape)))

    z_at = jnp.reshape(lax.axis_index("seq") // ys, (1,)).astype(jnp.int32)
    part_shape = shape_of(tile_dev, rows, 128)

    def pack_apart(first, second):
        return pl.pallas_call(
            pack_apart_kernel,
            out_shape=(part_shape,) * zs,
            in_specs=smem(1) + hbm(2),
            out_specs=hbm(zs),
            scratch_shapes=[scratch(tile_shape), scratch(tile_shape), scratch(head_shape), pltpu.SemaphoreType.DMA((zs,))],
            compiler_params=limits(16),
        )(z_at, pin(first.reshape(tile_shape.shape)), pin(second.reshape(tile_shape.shape)))

    def unpack_apart(parts):
        first, second = pl.pallas_call(
            unpack_apart_kernel,
            out_shape=(tile_shape, tile_shape),
            in_specs=smem(1) + hbm(zs),
            out_specs=hbm(2),
            scratch_shapes=[scratch(head_shape), scratch(tile_shape), scratch(tile_shape), pltpu.SemaphoreType.DMA((zs,))],
            compiler_params=limits(16),
        )(z_at, *map(pin, parts))
        return (
            first.reshape(1, tile_dev, 1, rows, width),
            second.reshape(1, tile_dev, 1, rows, width),
        )

    def shift_z(source, shift):
        pairs = [(z * ys + y, ((z + shift) % zs) * ys + y) for z in range(zs) for y in range(ys)]
        return lax.ppermute(source, "seq", pairs)

    def unpack(joined):
        first, second = pl.pallas_call(
            unpack_kernel,
            out_shape=(tile_shape, tile_shape),
            in_specs=hbm(1),
            out_specs=hbm(2),
            scratch_shapes=[scratch(head_shape), scratch(tile_shape), scratch(tile_shape), pltpu.SemaphoreType.DMA((3,))],
            compiler_params=limits(16),
        )(joined.reshape(head_shape.shape))
        return (
            first.reshape(1, tile_dev, 1, rows, width),
            second.reshape(1, tile_dev, 1, rows, width),
        )

    def over_z(source):
        return lax.all_to_all(
            source.reshape(head_shape.shape),
            "seq",
            split_axis=0,
            concat_axis=0,
            tiled=True,
            axis_index_groups=z_groups,
        ).reshape(block_shape.shape)

    def over_groups(source):
        return lax.all_to_all(source, "grp", split_axis=0, concat_axis=0, tiled=True)

    def over_y(source, shift):
        pairs = [(z * ys + y, z * ys + (y + shift) % ys) for z in range(zs) for y in range(ys)]
        return lax.ppermute(source, "seq", pairs)

    kv = over_z(pack(key_input, value_input))
    qg = list(pack_apart(queries, grad_output))
    first_rank, *qg = lax.optimization_barrier((far_rank, *qg))
    near_kv = [kv] + [over_y(kv, -shift) for shift in range(1, ys)]
    far_send = pl.pallas_call(
        functools.partial(far_kernel, far=far, zs=zs, tile_dev=tile_dev),
        out_shape=far_shape,
        in_specs=smem(1) + hbm(1),
        out_specs=hbm(1)[0],
        scratch_shapes=[pltpu.SemaphoreType.DMA],
        compiler_params=limits(8),
    )(first_rank, kv)
    far_kv = over_groups(far_send)
    qg[1:] = [shift_z(qg[shift], shift) for shift in range(1, zs)]

    slots = near + far + 1
    parts = pl.pallas_call(
        functools.partial(attend_kernel, tiles=tiles, entries=entries, ys=ys, zs=zs, far=far),
        out_shape=(part_shape,) * zs + (block_shape,) * ys + (far_shape,),
        in_specs=smem(3) + hbm(ys + 1 + zs),
        out_specs=hbm(ys + 1 + zs),
        scratch_shapes=[
            pltpu.VMEM((slots, rows, 128), bf16),
            pltpu.VMEM((slots, rows, 128), jnp.float32),
            pltpu.VMEM((3 * entries, rows, rows), jnp.float32),
            pltpu.VMEM((3 * entries, rows, rows), jnp.float32),
            pltpu.VMEM((3, rows, rows), jnp.float32),
            scratch(block_shape),
            pltpu.SemaphoreType.DMA((ys + 1 + zs,)),
        ],
        compiler_params=limits(48),
    )(code, count, z_at, kv, *map(pin, near_kv[1:]), far_kv, *map(pin, qg))
    odq, dkv_parts = list(parts[:zs]), parts[zs:]

    near_back = [dkv_parts[0]] + [over_y(dkv_parts[shift], shift) for shift in range(1, ys)]
    far_back = over_groups(dkv_parts[ys])
    odq[1:] = [shift_z(odq[shift], shift) for shift in range(1, zs)]
    last_rank, *odq[1:] = lax.optimization_barrier((far_rank, *odq[1:]))
    dkv = pl.pallas_call(
        functools.partial(combine_kernel, ys=ys, groups=groups, zs=zs, tile_dev=tile_dev),
        out_shape=block_shape,
        in_specs=smem(1) + hbm(ys + 1),
        out_specs=hbm(1)[0],
        scratch_shapes=[
            pltpu.VMEM((ys, tiles, rows, 128), bf16),
            pltpu.VMEM((groups, zs, rows, 128), bf16),
            scratch(block_shape, jnp.float32),
            pltpu.SemaphoreType.DMA((2, ys + 2)),
        ],
        compiler_params=limits(24),
    )(last_rank, *map(pin, near_back), far_back.reshape(groups, zs, rows, 128))
    attended, grad_queries = unpack_apart(odq)
    grad_keys, grad_values = unpack(over_z(dkv))
    return attended, grad_queries, grad_keys, grad_values


def solution(mesh):
    spec = P("grp", None, "seq", None, None)
    return jax.shard_map(
        per_device,
        mesh=mesh,
        in_specs=(spec, spec, spec, spec, P(), P()),
        out_specs=(spec, spec, spec, spec),
        check_vma=False,
    )
```
